256 devices in a mesh: ctx: 32 (over z, y), head: 8 (over x, core).
Axes of the slice: x: 4, y: 4, z: 8, core: 2. Of those that a mesh axis runs over, the one named last changes fastest.
Arguments:
- queries: bfloat16 [2048, 2048], P(None, 'head'), may hold values from -16 to 16
- prefix_keys: bfloat16 [32768, 2048], P('ctx', 'head'), may hold values from -6 to 6
- prefix_values: bfloat16 [32768, 2048], P('ctx', 'head'), may hold values from -6 to 6
- out_grad: bfloat16 [2048, 2048], P(None, 'head'), may hold values from -6 to 6
- block_lists: int32 [16, 16, 64], P('head'), may hold values from 0 to 511, as said below
- list_counts: int32 [16, 16], P('head'), may hold values from 32 to 64
Outputs:
- query_grad: bfloat16 [2048, 2048], P('ctx', 'head')
- key_grad: bfloat16 [32768, 2048], P(('ctx', 'head'))
- value_grad: bfloat16 [32768, 2048], P(('ctx', 'head'))
The draws below stay inside these ranges and needn't reach their ends.
Inputs may be any that keep to these rules, and one draw needn't show every extreme that they name: `block_lists`: within a list all 64 entries are distinct block numbers; entries from list_counts on are ignored. Of the live entries of every list at most 8 lie in the blocks of one context slice (slice c holds blocks c * 16 onward), and exactly 8 in one slice.
All inputs are finite; a program needn't handle non-finite values.
Results may differ from the reference program's by a relative error of at most 0.017.
Values may be sent and summed in bfloat16 or wider, within the bound.
A program may use at most 128 MiB of HBM per device.

```python
import jax
import jax.numpy as jnp
from jax import lax

H = 16
HD = 128
L = 2048
TILE = 128
BLOCK = 64
CTX_DEV = 1024
SEL = 64
MOST = 8
TILES = 16
TOKENS = 32768
N_CTX = 32


def draw_queries(key, part):
    sample = jax.random.normal(jax.random.fold_in(key, 1), (L, H * HD), jnp.float32)
    sample = jnp.clip(sample, -6.0, 6.0)
    return sample.astype(jnp.bfloat16)


def draw_prefix_keys(key, part):
    sample = jnp.clip(jax.random.normal(jax.random.fold_in(key, 3), (TOKENS, H * HD), jnp.float32), -6.0, 6.0)
    return sample.astype(jnp.bfloat16)


def list_tables(key):
    blocks_here = CTX_DEV // BLOCK
    list_total = H * TILES
    list_keys = jax.random.split(jax.random.fold_in(key, 7), list_total)
    spread = SEL - MOST

    def one_list(list_key, list_index):
        busiest = jax.random.randint(jax.random.fold_in(list_key, 1), (), 0, N_CTX)
        offset_draw = jax.random.randint(jax.random.fold_in(list_key, 2), (), 0, N_CTX - 1)
        order_draw = jax.random.randint(jax.random.fold_in(list_key, 3), (N_CTX, blocks_here), 0, 1 << 20)
        orders = jnp.argsort(order_draw * blocks_here + jnp.arange(blocks_here, dtype=jnp.int32)[None, :], axis=1).astype(jnp.int32)
        entry_pos = jnp.arange(spread, dtype=jnp.int32)
        device_rest = (busiest + 1 + (entry_pos + offset_draw) % (N_CTX - 1)) % N_CTX
        rank_rest = entry_pos // (N_CTX - 1)
        device_of = jnp.concatenate([jnp.full((MOST,), busiest, jnp.int32), device_rest.astype(jnp.int32)])
        rank_of = jnp.concatenate([jnp.arange(MOST, dtype=jnp.int32), rank_rest.astype(jnp.int32)])
        local_block = orders[device_of, rank_of]
        entries = device_of * blocks_here + local_block
        drawn_count = jax.random.randint(jax.random.fold_in(list_key, 4), (), max(MOST, SEL // 2), SEL + 1)
        list_count = jnp.where(list_index == 0, SEL, drawn_count).astype(jnp.int32)
        slots = jnp.arange(SEL, dtype=jnp.int32)
        shuffle_draw = jax.random.randint(jax.random.fold_in(list_key, 5), (SEL,), 0, 1 << 16)
        sort_scores = jnp.where(slots < list_count, shuffle_draw * SEL + slots, (1 << 22) + slots)
        reorder = jnp.argsort(sort_scores)
        return (entries[reorder].astype(jnp.int32), list_count)
    entries, list_counts = jax.vmap(one_list)(list_keys, jnp.arange(list_total, dtype=jnp.int32))
    return (entries.reshape(H, TILES, SEL), list_counts.reshape(H, TILES))


def draw_block_lists(key, part):
    return list_tables(key)[0]


def draw_list_counts(key, part):
    return list_tables(key)[1]


def levels(stream_key, shape, cuts, least, high):
    loudness = 1.0
    for dim, shards_of in cuts:
        steps = jax.random.uniform(jax.random.fold_in(jax.random.fold_in(stream_key, 6), dim), (shards_of,), jnp.float32, least / len(cuts), high / len(cuts))
        loudness = loudness * jnp.repeat(jnp.exp(steps), shape[dim] // shards_of).reshape((-1,) + (1,) * (len(shape) - 1 - dim))
    return loudness


def centred(own_key, dims, deviation, bound, pieces=(), kind=jnp.bfloat16):
    array = jax.random.normal(own_key, dims, jnp.float32) * deviation
    if len(pieces) > 0:
        array = levels(own_key, dims, pieces, -0.22, 0.18) * array
    return jnp.clip(array, min=-bound, max=bound).astype(kind)


def setup_inputs(seed: int = 0) -> dict:
    keys = jax.random.split(jax.random.key(seed), 7)
    return {
        "queries": draw_queries(jax.random.fold_in(keys[6], 71), 0),
        "prefix_keys": draw_prefix_keys(jax.random.fold_in(keys[6], 71), 0),
        "prefix_values": centred(keys[2], (TOKENS, H * HD), 1.0, 6.0, ((0, 32), (1, 8))),
        "out_grad": centred(keys[3], (L, H * HD), 1.0, 6.0, ((1, 8),)),
        "block_lists": draw_block_lists(jax.random.fold_in(keys[6], 71), 0),
        "list_counts": draw_list_counts(jax.random.fold_in(keys[6], 71), 0),
    }


masked_score = -1.0e30


def head_pass(query_head, key_head, value_head, grad_head, head_lists, head_counts):
    score_scale = HD ** -0.5
    offsets = jnp.arange(BLOCK, dtype=jnp.int32)
    positions = jnp.arange(SEL, dtype=jnp.int32)

    def tile_step(accum, tile_item):
        key_accum, value_accum = accum
        query_tile, grad_tile, picked, list_count = tile_item
        token_rows = (picked[:, None] * BLOCK + offsets[None, :]).reshape(-1).astype(jnp.int32)
        listed = jnp.repeat(positions < list_count, BLOCK)
        key_set = jnp.take(key_head, token_rows, axis=0)
        value_set = jnp.take(value_head, token_rows, axis=0)
        scores = score_scale * jnp.dot(query_tile, key_set.T, preferred_element_type=jnp.float32)
        scores = jnp.where(listed[None, :], scores, masked_score)
        row_max = jnp.max(scores, axis=1, keepdims=True)
        row_total = jnp.sum(jnp.where(listed[None, :], jnp.exp(scores - row_max), 0.0), axis=1, keepdims=True)
        log_total = row_max + jnp.log(row_total)
        attn_probs = jnp.where(listed[None, :], jnp.exp(scores - log_total), 0.0)
        dprobs = jnp.dot(grad_tile, value_set.T, preferred_element_type=jnp.float32)
        row_delta = jnp.sum(attn_probs * dprobs, axis=1, keepdims=True)
        dscores = (attn_probs * (dprobs - row_delta)).astype(jnp.bfloat16)
        probs_low = attn_probs.astype(jnp.bfloat16)
        query_part = score_scale * jnp.dot(dscores, key_set, preferred_element_type=jnp.float32)
        key_part = score_scale * jnp.dot(dscores.T, query_tile, preferred_element_type=jnp.float32)
        value_part = jnp.dot(probs_low.T, grad_tile, preferred_element_type=jnp.float32)
        key_accum = key_accum.at[token_rows].add(key_part)
        value_accum = value_accum.at[token_rows].add(value_part)
        return (key_accum, value_accum), query_part.astype(jnp.bfloat16)

    start_accum = (jnp.zeros((TOKENS, HD), jnp.float32), jnp.zeros((TOKENS, HD), jnp.float32))
    tile_items = (query_head.reshape(TILES, TILE, HD), grad_head.reshape(TILES, TILE, HD), head_lists, head_counts)
    final_accum, query_tiles = lax.scan(tile_step, start_accum, tile_items)
    return (query_tiles.reshape(L, HD), final_accum[0].astype(jnp.bfloat16), final_accum[1].astype(jnp.bfloat16))


def reference(queries, prefix_keys, prefix_values, out_grad, block_lists, list_counts):
    def one_head(head_index):
        first_col = (head_index * HD).astype(jnp.int32)

        def pick_cols(source):
            return lax.dynamic_slice_in_dim(source, first_col, HD, 1)

        return head_pass(pick_cols(queries), pick_cols(prefix_keys), pick_cols(prefix_values), pick_cols(out_grad), block_lists[head_index], list_counts[head_index])

    query_parts, key_parts, value_parts = lax.map(one_head, jnp.arange(H, dtype=jnp.int32))
    query_grad = jnp.transpose(query_parts, (1, 0, 2)).reshape(L, H * HD)
    key_grad = jnp.transpose(key_parts, (1, 0, 2)).reshape(TOKENS, H * HD)
    value_grad = jnp.transpose(value_parts, (1, 0, 2)).reshape(TOKENS, H * HD)
    return (query_grad, key_grad, value_grad)
```

```python
import functools

import jax
import jax.numpy as jnp
from jax import lax
from jax.experimental import pallas as pl
from jax.experimental.pallas import tpu as pltpu
from jax.sharding import PartitionSpec as P

HD = 128
TILE = 128
BLOCK = 64
MOST = 8
NEAR = 2
Y = 4
MASKED = -1e30
SCALE = HD ** -0.5
SCALE2 = SCALE * 1.4426950408889634
MESH = pl.DeviceIdType.MESH
F32 = jnp.float32
BF16 = jnp.bfloat16
VMEM_LIMIT = 48 * 1024 * 1024


def dot_nt(a, b):
    return lax.dot_general(a, b, (((1,), (1,)), ((), ())), preferred_element_type=F32)


def dot_nn(a, b):
    return lax.dot_general(a, b, (((1,), (0,)), ((), ())), preferred_element_type=F32)


def dot_tn(a, b):
    return lax.dot_general(a, b, (((0,), (0,)), ((), ())), preferred_element_type=F32)


def picked(ref, table, row, head, first, slots):
    cols = pl.ds(head * HD, HD)
    parts = []
    for slot in range(first, first + slots):
        start = pl.multiple_of(table[row, slot] * BLOCK, BLOCK)
        parts.append(ref[pl.ds(start, BLOCK), cols])
    return jnp.concatenate(parts, axis=0)


def slot_table(lists, counts_row, me, blocks_here):
    tiles, sel = lists.shape
    eye = lax.broadcasted_iota(jnp.int32, (tiles, tiles), 0) == lax.broadcasted_iota(jnp.int32, (tiles, tiles), 1)
    counts = jnp.sum(jnp.where(eye, counts_row, 0), axis=1, keepdims=True)
    local = lists - me * blocks_here
    pos = lax.broadcasted_iota(jnp.int32, (tiles, sel), 1)
    listed = (pos < counts) & (local >= 0) & (local < blocks_here)
    flags = jnp.where(listed, 1.0, 0.0)
    before = lax.broadcasted_iota(jnp.int32, (sel, sel), 0) < lax.broadcasted_iota(jnp.int32, (sel, sel), 1)
    rank = dot_nn(flags.astype(BF16), jnp.where(before, 1.0, 0.0).astype(BF16))
    ids = local.astype(F32)
    lane = lax.broadcasted_iota(jnp.int32, (tiles, 128), 1)
    total = jnp.sum(flags, axis=1, keepdims=True)
    table = jnp.where(lane == MOST, total, 0.0)
    for slot in range(MOST):
        value = jnp.sum(jnp.where(listed & (rank == float(slot)), ids, 0.0), axis=1, keepdims=True)
        table = jnp.where(lane == slot, value, table)
    return table.astype(jnp.int32)


def stats_kernel(heads, tiles, unroll, lists_ref, counts_ref, q_ref, k_ref, v_ref, g_ref, stats_ref, table_out, table_vmem, table, sem):
    me = lax.axis_index("ctx")
    blocks_here = k_ref.shape[0] // BLOCK
    for head in range(heads):
        table_vmem[pl.ds(head * tiles, tiles), :] = slot_table(
            lists_ref[head], counts_ref[pl.ds(head, 1), :], me, blocks_here
        )
    copy = pltpu.make_async_copy(table_vmem, table, sem)
    copy.start()
    table_out[...] = table_vmem[...]
    copy.wait()

    def part(head, tile, first, slots):
        row = head * tiles + tile
        live = (table[row, MOST] - first) * BLOCK
        rows = pl.ds(pl.multiple_of(tile * TILE, TILE), TILE)
        cols = pl.ds(head * HD, HD)
        keys = picked(k_ref, table, row, head, first, slots)
        vals = picked(v_ref, table, row, head, first, slots)
        scores = dot_nt(keys, q_ref[rows, cols]) * SCALE2
        dprobs = dot_nt(vals, g_ref[rows, cols])
        mask = lax.broadcasted_iota(jnp.int32, scores.shape, 0) < live
        scores = jnp.where(mask, scores, MASKED)
        top = jnp.max(scores, axis=0, keepdims=True)
        weights = jnp.where(mask, jnp.exp2(scores - top), 0.0)
        total = jnp.sum(weights, axis=0, keepdims=True)
        delta = jnp.sum(weights * dprobs, axis=0, keepdims=True)
        return top, total, delta

    def near(step, carry):
        for inner in range(unroll):
            for head in range(heads):
                tile = step * unroll + inner
                row = head * tiles + tile
                top, total, delta = part(head, tile, 0, NEAR)
                stats_ref[row, pl.ds(0, 1), :] = top
                stats_ref[row, pl.ds(1, 1), :] = total
                stats_ref[row, pl.ds(2, 1), :] = delta
        return carry

    lax.fori_loop(0, tiles // unroll, near, 0)

    def far(tile, carry):
        for head in range(heads):
            row = head * tiles + tile

            @pl.when(table[row, MOST] > NEAR)
            def _():
                top, total, delta = part(head, tile, NEAR, MOST - NEAR)
                old = stats_ref[row, pl.ds(0, 1), :]
                joint = jnp.maximum(old, top)
                a = jnp.exp2(old - joint)
                b = jnp.exp2(top - joint)
                stats_ref[row, pl.ds(0, 1), :] = joint
                stats_ref[row, pl.ds(1, 1), :] = a * stats_ref[row, pl.ds(1, 1), :] + b * total
                stats_ref[row, pl.ds(2, 1), :] = a * stats_ref[row, pl.ds(2, 1), :] + b * delta

        return carry

    lax.fori_loop(0, tiles, far, 0)


def join_kernel(n, stats_ref, out_ref, recv, merged, send1, recv1, send2, recv2):
    me = lax.axis_index("ctx")
    head = lax.axis_index("head")
    barrier = pltpu.get_barrier_semaphore()

    def greet(step, carry):
        peer = lax.rem(me + step, n)
        pl.semaphore_signal(barrier, inc=1, device_id=(peer, head), device_id_type=MESH)
        return carry

    lax.fori_loop(1, n, greet, 0)
    pl.semaphore_wait(barrier, n - 1)

    def first(peer, source):
        return pltpu.make_async_remote_copy(
            src_ref=stats_ref.at[peer], dst_ref=recv.at[source], send_sem=send1.at[peer], recv_sem=recv1.at[source],
            device_id=(peer, head), device_id_type=MESH,
        )

    def second(peer, source):
        return pltpu.make_async_remote_copy(
            src_ref=merged.at[source], dst_ref=merged.at[source], send_sem=send2.at[peer], recv_sem=recv2.at[source],
            device_id=(peer, head), device_id_type=MESH,
        )

    def over(body):
        def step(i, carry):
            body(lax.rem(me + i, n))
            return carry

        lax.fori_loop(1, n, step, 0)

    over(lambda peer: first(peer, me).start())
    recv[me] = stats_ref[me]
    over(lambda peer: first(peer, peer).wait_recv())
    pieces = recv[...]
    tops = pieces[:, 0, :]
    top = jnp.max(tops, axis=0, keepdims=True)
    share = jnp.exp2(tops - top)
    total = jnp.sum(share * pieces[:, 1, :], axis=0, keepdims=True)
    delta = jnp.sum(share * pieces[:, 2, :], axis=0, keepdims=True)
    merged[me, pl.ds(0, 1), :] = top + jnp.log2(total)
    merged[me, pl.ds(1, 1), :] = delta / total
    over(lambda peer: second(peer, me).start())
    over(lambda peer: first(peer, me).wait_send())
    over(lambda peer: second(peer, peer).wait_recv())
    out_ref[...] = merged[...]
    over(lambda peer: second(peer, me).wait_send())


def grads_kernel(heads, tiles, unroll, table, stats_ref, q_ref, k_ref, v_ref, g_ref, dq_ref, dk_ref, dv_ref, dk_acc, dv_acc):
    dk_acc[...] = jnp.zeros_like(dk_acc)
    dv_acc[...] = jnp.zeros_like(dv_acc)

    def part(head, tile, first, slots):
        row = head * tiles + tile
        live = (table[row, MOST] - first) * BLOCK
        rows = pl.ds(pl.multiple_of(tile * TILE, TILE), TILE)
        cols = pl.ds(head * HD, HD)
        keys = picked(k_ref, table, row, head, first, slots)
        vals = picked(v_ref, table, row, head, first, slots)
        query = q_ref[rows, cols]
        grad = g_ref[rows, cols]
        scores = dot_nt(keys, query) * SCALE2
        dprobs = dot_nt(vals, grad)
        mask = lax.broadcasted_iota(jnp.int32, scores.shape, 0) < live
        log_total = stats_ref[row, pl.ds(0, 1), :]
        delta = stats_ref[row, pl.ds(1, 1), :]
        probs = jnp.where(mask, jnp.exp2(scores - log_total), 0.0)
        dscores = (probs * (dprobs - delta)).astype(BF16)
        low = probs.astype(BF16)
        dkeys = dot_nn(dscores, query)
        dvals = dot_nn(low, grad)
        dquery = dot_tn(dscores, keys) * SCALE
        for slot in range(slots):
            start = pl.multiple_of(table[row, first + slot] * BLOCK, BLOCK)
            dk_acc[head, pl.ds(start, BLOCK), :] += dkeys[slot * BLOCK : (slot + 1) * BLOCK]
            dv_acc[head, pl.ds(start, BLOCK), :] += dvals[slot * BLOCK : (slot + 1) * BLOCK]
        return dquery

    def near(step, carry):
        for inner in range(unroll):
            for head in range(heads):
                tile = step * unroll + inner
                rows = pl.ds(pl.multiple_of(tile * TILE, TILE), TILE)
                dq_ref[rows, pl.ds(head * HD, HD)] = part(head, tile, 0, NEAR).astype(BF16)
        return carry

    lax.fori_loop(0, tiles // unroll, near, 0)

    def far(tile, carry):
        for head in range(heads):
            row = head * tiles + tile

            @pl.when(table[row, MOST] > NEAR)
            def _():
                rows = pl.ds(pl.multiple_of(tile * TILE, TILE), TILE)
                cols = pl.ds(head * HD, HD)
                extra = part(head, tile, NEAR, MOST - NEAR)
                dq_ref[rows, cols] = (dq_ref[rows, cols].astype(F32) + extra).astype(BF16)

        return carry

    lax.fori_loop(0, tiles, far, 0)
    for head in range(heads):
        cols = pl.ds(head * HD, HD)
        dk_ref[:, cols] = (dk_acc[head] * SCALE).astype(BF16)
        dv_ref[:, cols] = dv_acc[head].astype(BF16)


def swap_kernel(n_ctx, n_head, dq_ref, dk_ref, dv_ref, oq_ref, ok_ref, ov_ref,
                ybuf, zsend, zbuf, ssend, srecv, ysend, yrecv, zsend_sem, zrecv, own):
    me = lax.axis_index("ctx")
    head = lax.axis_index("head")
    n_z = n_ctx // Y
    z = me // Y
    y = lax.rem(me, Y)
    tokens = ok_ref.shape[0]
    width = dk_ref.shape[1]
    barrier = pltpu.get_barrier_semaphore()

    def at_head(i):
        return (me, lax.rem(head + i, n_head))

    def at_y(i):
        return (z * Y + lax.rem(y + i, Y), head)

    def at_z(i):
        return (lax.rem(z + i, n_z) * Y + y, head)

    for count, where in ((n_head, at_head), (Y, at_y), (n_z, at_z)):
        for i in range(1, count):
            pl.semaphore_signal(barrier, inc=1, device_id=where(i), device_id_type=MESH)
    pl.semaphore_wait(barrier, n_head + Y + n_z - 3)

    def token_copy(which, i, source):
        src, dst = ((dk_ref, ok_ref), (dv_ref, ov_ref))[which]
        peer = lax.rem(head + i, n_head)
        return pltpu.make_async_remote_copy(
            src_ref=src.at[pl.ds(pl.multiple_of(peer * tokens, tokens), tokens), :],
            dst_ref=dst.at[:, pl.ds(pl.multiple_of(source * width, width), width)],
            send_sem=ssend.at[which, i], recv_sem=srecv.at[which, source],
            device_id=(me, peer), device_id_type=MESH,
        )

    def y_copy(zz, i, source):
        peer = lax.rem(y + i, Y)
        return pltpu.make_async_remote_copy(
            src_ref=dq_ref.at[zz, peer], dst_ref=ybuf.at[zz, source],
            send_sem=ysend.at[zz, i], recv_sem=yrecv.at[zz, source],
            device_id=(z * Y + peer, head), device_id_type=MESH,
        )

    def z_copy(i, source):
        peer = lax.rem(z + i, n_z)
        return pltpu.make_async_remote_copy(
            src_ref=zsend.at[peer], dst_ref=zbuf.at[source],
            send_sem=zsend_sem.at[i], recv_sem=zrecv.at[source],
            device_id=(peer * Y + y, head), device_id_type=MESH,
        )

    for i in range(1, n_z + 1):
        zz = lax.rem(z + i, n_z)
        for j in (2, 1, 3):
            y_copy(zz, j, y).start()
    for i in range(1, n_head):
        for which in range(2):
            token_copy(which, i, head).start()
    mine = []
    for which in range(2):
        src, dst = ((dk_ref, ok_ref), (dv_ref, ov_ref))[which]
        copy = pltpu.make_async_copy(
            src.at[pl.ds(pl.multiple_of(head * tokens, tokens), tokens), :],
            dst.at[:, pl.ds(pl.multiple_of(head * width, width), width)],
            own.at[which],
        )
        copy.start()
        mine.append(copy)

    for i in range(1, n_z + 1):
        zz = lax.rem(z + i, n_z)
        total = dq_ref[zz, y].astype(F32)
        for j in range(1, Y):
            source = lax.rem(y + j, Y)
            y_copy(zz, j, source).wait_recv()
            total = total + ybuf[zz, source].astype(F32)
        if i < n_z:
            zsend[zz] = total.astype(BF16)
            z_copy(i, z).start()
    for i in range(1, n_z):
        source = lax.rem(z + i, n_z)
        z_copy(i, source).wait_recv()
        total = total + zbuf[source].astype(F32)
    oq_ref[...] = total.astype(BF16)
    for copy in mine:
        copy.wait()
    for i in range(1, n_head):
        for which in range(2):
            token_copy(which, i, lax.rem(head + i, n_head)).wait_recv()
    for i in range(1, n_z + 1):
        zz = lax.rem(z + i, n_z)
        for j in range(1, Y):
            y_copy(zz, j, y).wait_send()
    for i in range(1, n_z):
        z_copy(i, z).wait_send()
    for i in range(1, n_head):
        for which in range(2):
            token_copy(which, i, head).wait_send()


def local(n_ctx, n_head, queries, prefix_keys, prefix_values, out_grad, block_lists, list_counts):
    latents, width = queries.shape
    tokens = prefix_keys.shape[0]
    heads = width // HD
    tiles = latents // TILE
    rows = heads * tiles
    n_z = n_ctx // Y
    own = latents // n_ctx
    vmem = pl.BlockSpec(memory_space=pltpu.VMEM)
    smem = pl.BlockSpec(memory_space=pltpu.SMEM)
    anyplace = pl.BlockSpec(memory_space=pl.ANY)
    stats, table = pl.pallas_call(
        functools.partial(stats_kernel, heads, tiles, 4),
        name="local_stats",
        out_shape=(jax.ShapeDtypeStruct((rows, 3, TILE), F32), jax.ShapeDtypeStruct((rows, 128), jnp.int32)),
        in_specs=[vmem] * 6,
        out_specs=(vmem, vmem),
        scratch_shapes=[pltpu.VMEM((rows, 128), jnp.int32), pltpu.SMEM((rows, 128), jnp.int32), pltpu.SemaphoreType.DMA],
        compiler_params=pltpu.CompilerParams(vmem_limit_bytes=VMEM_LIMIT),
    )(block_lists, list_counts, queries, prefix_keys, prefix_values, out_grad)
    totals = pl.pallas_call(
        functools.partial(join_kernel, n_ctx),
        name="join_stats",
        out_shape=jax.ShapeDtypeStruct((rows, 2, TILE), F32),
        in_specs=[vmem],
        out_specs=vmem,
        scratch_shapes=[
            pltpu.VMEM((n_ctx, 3, TILE), F32),
            pltpu.VMEM((n_ctx, 2, TILE), F32),
            pltpu.SemaphoreType.DMA((n_ctx,)),
            pltpu.SemaphoreType.DMA((n_ctx,)),
            pltpu.SemaphoreType.DMA((n_ctx,)),
            pltpu.SemaphoreType.DMA((n_ctx,)),
        ],
        compiler_params=pltpu.CompilerParams(collective_id=0, has_side_effects=True),
    )(stats)
    dq, dk, dv = pl.pallas_call(
        functools.partial(grads_kernel, heads, tiles, 4),
        name="local_grads",
        out_shape=(
            jax.ShapeDtypeStruct((latents, width), BF16),
            jax.ShapeDtypeStruct((tokens, width), BF16),
            jax.ShapeDtypeStruct((tokens, width), BF16),
        ),
        in_specs=[smem] + [vmem] * 5,
        out_specs=(vmem, vmem, vmem),
        scratch_shapes=[pltpu.VMEM((heads, tokens, HD), F32), pltpu.VMEM((heads, tokens, HD), F32)],
        compiler_params=pltpu.CompilerParams(vmem_limit_bytes=VMEM_LIMIT),
    )(table, totals, queries, prefix_keys, prefix_values, out_grad)
    piece = tokens // n_head
    return pl.pallas_call(
        functools.partial(swap_kernel, n_ctx, n_head),
        name="swap_grads",
        out_shape=(
            jax.ShapeDtypeStruct((own, width), BF16),
            jax.ShapeDtypeStruct((piece, n_head * width), BF16),
            jax.ShapeDtypeStruct((piece, n_head * width), BF16),
        ),
        in_specs=[vmem, vmem, vmem],
        out_specs=(vmem, vmem, vmem),
        scratch_shapes=[
            pltpu.VMEM((n_z, Y, own, width), BF16),
            pltpu.VMEM((n_z, own, width), BF16),
            pltpu.VMEM((n_z, own, width), BF16),
            pltpu.SemaphoreType.DMA((2, n_head)),
            pltpu.SemaphoreType.DMA((2, n_head)),
            pltpu.SemaphoreType.DMA((n_z, Y)),
            pltpu.SemaphoreType.DMA((n_z, Y)),
            pltpu.SemaphoreType.DMA((n_z,)),
            pltpu.SemaphoreType.DMA((n_z,)),
            pltpu.SemaphoreType.DMA((2,)),
        ],
        compiler_params=pltpu.CompilerParams(collective_id=1, has_side_effects=True, vmem_limit_bytes=VMEM_LIMIT),
    )(dq.reshape(n_z, Y, own, width), dk, dv)


def solution(mesh):
    return jax.shard_map(
        functools.partial(local, mesh.shape["ctx"], mesh.shape["head"]),
        mesh=mesh,
        in_specs=(
            P(None, "head"),
            P("ctx", "head"),
            P("ctx", "head"),
            P(None, "head"),
            P("head", None, None),
            P("head", None),
        ),
        out_specs=(P("ctx", "head"), P(("ctx", "head"), None), P(("ctx", "head"), None)),
        check_vma=False,
    )
```

```python
import functools

import jax
import jax.numpy as jnp
from jax import lax
from jax.experimental import pallas as pl
from jax.experimental.pallas import tpu as pltpu
from jax.sharding import PartitionSpec as P

HD = 128
TILE = 128
BLOCK = 64
MOST = 8
NEAR = 2
Y = 4
GROUP = 4
MASKED = -1e30
SCALE = HD ** -0.5
SCALE2 = SCALE * 1.4426950408889634
MESH = pl.DeviceIdType.MESH
F32 = jnp.float32
BF16 = jnp.bfloat16
VMEM_LIMIT = 16 * 1024 * 1024


def dot_nt(a, b):
    return lax.dot_general(a, b, (((1,), (1,)), ((), ())), preferred_element_type=F32)


def dot_nn(a, b):
    return lax.dot_general(a, b, (((1,), (0,)), ((), ())), preferred_element_type=F32)


def dot_tn(a, b):
    return lax.dot_general(a, b, (((0,), (0,)), ((), ())), preferred_element_type=F32)


def picked(ref, table, row, head, first, slots):
    cols = pl.ds(head * HD, HD)
    parts = []
    for slot in range(first, first + slots):
        start = pl.multiple_of(table[row, slot] * BLOCK, BLOCK)
        parts.append(ref[pl.ds(start, BLOCK), cols])
    return jnp.concatenate(parts, axis=0)


def slot_table(lists, counts_row, me, blocks_here):
    tiles, sel = lists.shape
    eye = lax.broadcasted_iota(jnp.int32, (tiles, tiles), 0) == lax.broadcasted_iota(jnp.int32, (tiles, tiles), 1)
    counts = jnp.sum(jnp.where(eye, counts_row, 0), axis=1, keepdims=True)
    local = lists - me * blocks_here
    pos = lax.broadcasted_iota(jnp.int32, (tiles, sel), 1)
    listed = (pos < counts) & (local >= 0) & (local < blocks_here)
    flags = jnp.where(listed, 1.0, 0.0)
    before = lax.broadcasted_iota(jnp.int32, (sel, sel), 0) < lax.broadcasted_iota(jnp.int32, (sel, sel), 1)
    rank = dot_nn(flags.astype(BF16), jnp.where(before, 1.0, 0.0).astype(BF16))
    ids = local.astype(F32)
    lane = lax.broadcasted_iota(jnp.int32, (tiles, 128), 1)
    total = jnp.sum(flags, axis=1, keepdims=True)
    table = jnp.where(lane == MOST, total, 0.0)
    for slot in range(MOST):
        value = jnp.sum(jnp.where(listed & (rank == float(slot)), ids, 0.0), axis=1, keepdims=True)
        table = jnp.where(lane == slot, value, table)
    return table.astype(jnp.int32)


def diagonal(a, b):
    zero = jnp.zeros_like(a)
    return jnp.concatenate([jnp.concatenate([a, zero], axis=1), jnp.concatenate([zero, b], axis=1)], axis=0)


def stats_kernel(heads, tiles, unroll, lists_hbm, counts_hbm, q_hbm, k_hbm, v_hbm, g_hbm,
                 stats_ref, table_out, tops_ref, weights_ref, dprobs_ref,
                 lists_ref, counts_ref, q_ref, k_ref, v_ref, g_ref, table, sem, table_sem):
    me = lax.axis_index("ctx")
    blocks_here = k_ref.shape[0] // BLOCK
    fetches = [
        pltpu.make_async_copy(source, target, sem.at[i])
        for i, (source, target) in enumerate(
            ((lists_hbm, lists_ref), (counts_hbm, counts_ref), (k_hbm, k_ref), (q_hbm, q_ref), (v_hbm, v_ref), (g_hbm, g_ref))
        )
    ]
    for fetch in fetches:
        fetch.start()
    fetches[0].wait()
    fetches[1].wait()
    for head in range(heads):
        table_out[pl.ds(head * tiles, tiles), :] = slot_table(
            lists_ref[head], counts_ref[pl.ds(head, 1), :], me, blocks_here
        )
    copy = pltpu.make_async_copy(table_out, table, table_sem)
    copy.start()
    copy.wait()
    for fetch in fetches[2:]:
        fetch.wait()

    def part(head, tile, first, slots):
        row = head * tiles + tile
        live = (table[row, MOST] - first) * BLOCK
        rows = pl.ds(pl.multiple_of(tile * TILE, TILE), TILE)
        cols = pl.ds(head * HD, HD)
        keys = picked(k_ref, table, row, head, first, slots)
        vals = picked(v_ref, table, row, head, first, slots)
        scores = dot_nt(keys, q_ref[rows, cols]) * SCALE2
        dprobs = dot_nt(vals, g_ref[rows, cols])
        mask = lax.broadcasted_iota(jnp.int32, scores.shape, 0) < live
        scores = jnp.where(mask, scores, MASKED)
        top = jnp.max(scores, axis=0, keepdims=True)
        weights = jnp.where(mask, jnp.exp2(scores - top), 0.0)
        total = jnp.sum(weights, axis=0, keepdims=True)
        delta = jnp.sum(weights * dprobs, axis=0, keepdims=True)
        return weights, dprobs, top, total, delta

    def near(step, carry):
        for inner in range(unroll):
            for head in range(heads):
                tile = step * unroll + inner
                row = head * tiles + tile
                group = head * (tiles // GROUP) + step * (unroll // GROUP) + inner // GROUP
                place = pl.ds(inner % GROUP, 1)
                weights, dprobs, top, total, delta = part(head, tile, 0, NEAR)
                weights_ref[row] = weights
                dprobs_ref[row] = dprobs
                tops_ref[group, place, :] = top
                stats_ref[group, 0, place, :] = top
                stats_ref[group, 1, place, :] = total
                stats_ref[group, 2, place, :] = delta
        return carry

    lax.fori_loop(0, tiles // unroll, near, 0)

    def far(step, carry):
        for inner in range(GROUP):
            for head in range(heads):
                tile = step * GROUP + inner
                row = head * tiles + tile
                group = head * (tiles // GROUP) + step
                place = pl.ds(inner, 1)

                @pl.when(table[row, MOST] > NEAR)
                def _():
                    _, _, top, total, delta = part(head, tile, NEAR, MOST - NEAR)
                    old = stats_ref[group, 0, place, :]
                    joint = jnp.maximum(old, top)
                    a = jnp.exp2(old - joint)
                    b = jnp.exp2(top - joint)
                    stats_ref[group, 0, place, :] = joint
                    stats_ref[group, 1, place, :] = a * stats_ref[group, 1, place, :] + b * total
                    stats_ref[group, 2, place, :] = a * stats_ref[group, 2, place, :] + b * delta

        return carry

    lax.fori_loop(0, tiles // GROUP, far, 0)


def join_kernel(n_ctx, stats_ref, out_ref, zbuf, ybuf, part, merged, send1, recv1, send2, recv2, send3, recv3):
    me = lax.axis_index("ctx")
    head = lax.axis_index("head")
    n_z = n_ctx // Y
    z = me // Y
    y = lax.rem(me, Y)
    far_first = sorted(range(1, n_z), key=lambda i: -min(i, n_z - i))
    barrier = pltpu.get_barrier_semaphore()
    for i in far_first:
        pl.semaphore_signal(barrier, inc=1, device_id=(lax.rem(z + i, n_z) * Y + y, head), device_id_type=MESH)
    for i in range(1, Y):
        pl.semaphore_signal(barrier, inc=1, device_id=(z * Y + lax.rem(y + i, Y), head), device_id_type=MESH)
    pl.semaphore_wait(barrier, n_z + Y - 2)

    def first(i, source):
        peer = lax.rem(z + i, n_z)
        return pltpu.make_async_remote_copy(
            src_ref=stats_ref.at[peer], dst_ref=zbuf.at[source], send_sem=send1.at[i], recv_sem=recv1.at[source],
            device_id=(peer * Y + y, head), device_id_type=MESH,
        )

    def second(i, source):
        peer = lax.rem(y + i, Y)
        return pltpu.make_async_remote_copy(
            src_ref=part, dst_ref=ybuf.at[source], send_sem=send2.at[i], recv_sem=recv2.at[source],
            device_id=(z * Y + peer, head), device_id_type=MESH,
        )

    def third(i, source):
        peer = lax.rem(z + i, n_z)
        return pltpu.make_async_remote_copy(
            src_ref=merged.at[source], dst_ref=merged.at[source], send_sem=send3.at[i], recv_sem=recv3.at[source],
            device_id=(peer * Y + y, head), device_id_type=MESH,
        )

    def combine(pieces):
        tops = pieces[:, 0]
        top = jnp.max(tops, axis=0)
        share = jnp.exp2(tops - top[None])
        return top, jnp.sum(share * pieces[:, 1], axis=0), jnp.sum(share * pieces[:, 2], axis=0)

    for i in far_first:
        first(i, z).start()
    zbuf[z] = stats_ref[z]
    for i in range(1, n_z):
        first(i, lax.rem(z + i, n_z)).wait_recv()
    for kind, value in enumerate(combine(zbuf[...])):
        part[kind] = value
    for i in (2, 1, 3):
        second(i, y).start()
    ybuf[y] = part[...]
    for i in range(1, Y):
        second(i, lax.rem(y + i, Y)).wait_recv()
    top, total, delta = combine(ybuf[...])
    merged[z, 0] = top + jnp.log2(total)
    merged[z, 1] = delta / total
    for i in far_first:
        third(i, z).start()
    for i in range(1, n_z):
        first(i, z).wait_send()
    for i in range(1, Y):
        second(i, y).wait_send()
    for i in range(1, n_z):
        third(i, lax.rem(z + i, n_z)).wait_recv()
    out_ref[...] = merged[...]
    for i in range(1, n_z):
        third(i, z).wait_send()


def grads_kernel(heads, tiles, unroll, table, totals_ref, tops_ref, weights_ref, dprobs_ref, q_ref, k_ref, v_ref, g_ref,
                 dq_ref, dk_ref, dv_ref, acc):
    acc[...] = jnp.zeros_like(acc)

    def spread(head, tile, group, place, first, probs, dprobs, keys):
        row = head * tiles + tile
        rows = pl.ds(pl.multiple_of(tile * TILE, TILE), TILE)
        cols = pl.ds(head * HD, HD)
        dscores = (probs * (dprobs - totals_ref[group, 1, place, :])).astype(BF16)
        both = jnp.concatenate([dscores, probs.astype(BF16)], axis=1)
        moved = dot_nn(both, diagonal(q_ref[rows, cols], g_ref[rows, cols]))
        for slot in range(keys.shape[0] // BLOCK):
            start = pl.multiple_of(table[row, first + slot] * BLOCK, BLOCK)
            acc[head, pl.ds(start, BLOCK), :] += moved[slot * BLOCK : (slot + 1) * BLOCK]
        return dscores

    def near(step, carry):
        for inner in range(unroll):
            tile = step * unroll + inner
            rows = pl.ds(pl.multiple_of(tile * TILE, TILE), TILE)
            place = pl.ds(inner % GROUP, 1)
            pieces = []
            for head in range(heads):
                row = head * tiles + tile
                group = head * (tiles // GROUP) + step * (unroll // GROUP) + inner // GROUP
                share = jnp.exp2(tops_ref[group, place, :] - totals_ref[group, 0, place, :])
                keys = picked(k_ref, table, row, head, 0, NEAR)
                dscores = spread(head, tile, group, place, 0, weights_ref[row] * share, dprobs_ref[row], keys)
                pieces.append((dscores, keys))
            moved = dot_tn(
                jnp.concatenate([pieces[0][0], pieces[1][0]], axis=0), diagonal(pieces[0][1], pieces[1][1])
            )
            dq_ref[rows, :] = (moved * SCALE).astype(BF16)
        return carry

    lax.fori_loop(0, tiles // unroll, near, 0)

    def far(step, carry):
        for inner in range(GROUP):
            for head in range(heads):
                tile = step * GROUP + inner
                row = head * tiles + tile
                group = head * (tiles // GROUP) + step
                place = pl.ds(inner, 1)

                @pl.when(table[row, MOST] > NEAR)
                def _():
                    rows = pl.ds(pl.multiple_of(tile * TILE, TILE), TILE)
                    cols = pl.ds(head * HD, HD)
                    live = (table[row, MOST] - NEAR) * BLOCK
                    keys = picked(k_ref, table, row, head, NEAR, MOST - NEAR)
                    vals = picked(v_ref, table, row, head, NEAR, MOST - NEAR)
                    scores = dot_nt(keys, q_ref[rows, cols]) * SCALE2
                    dprobs = dot_nt(vals, g_ref[rows, cols])
                    mask = lax.broadcasted_iota(jnp.int32, scores.shape, 0) < live
                    probs = jnp.where(mask, jnp.exp2(scores - totals_ref[group, 0, place, :]), 0.0)
                    dscores = spread(head, tile, group, place, NEAR, probs, dprobs, keys)
                    extra = dot_tn(dscores, keys) * SCALE
                    dq_ref[rows, cols] = (dq_ref[rows, cols].astype(F32) + extra).astype(BF16)

        return carry

    lax.fori_loop(0, tiles // GROUP, far, 0)
    for head in range(heads):
        cols = pl.ds(head * HD, HD)
        dk_ref[:, cols] = (acc[head, :, pl.ds(0, HD)] * SCALE).astype(BF16)
        dv_ref[:, cols] = acc[head, :, pl.ds(HD, HD)].astype(BF16)


def leave_kernel(count, *refs):
    sem = refs[2 * count]
    copies = [pltpu.make_async_copy(refs[i], refs[count + i], sem.at[i]) for i in range(count)]
    for copy in copies:
        copy.start()
    for copy in copies:
        copy.wait()


def swap_kernel(n_ctx, n_head, dq_ref, dk_ref, dv_ref, oq_ref, ok_ref, ov_ref,
                ybuf, zsend, zbuf, ssend, srecv, ysend, yrecv, zsend_sem, zrecv, own):
    me = lax.axis_index("ctx")
    head = lax.axis_index("head")
    n_z = n_ctx // Y
    z = me // Y
    y = lax.rem(me, Y)
    tokens = ok_ref.shape[0]
    width = dk_ref.shape[1]
    barrier = pltpu.get_barrier_semaphore()

    def at_head(i):
        return (me, lax.rem(head + i, n_head))

    def at_y(i):
        return (z * Y + lax.rem(y + i, Y), head)

    def at_z(i):
        return (lax.rem(z + i, n_z) * Y + y, head)

    for count, where in ((n_head, at_head), (Y, at_y), (n_z, at_z)):
        for i in range(1, count):
            pl.semaphore_signal(barrier, inc=1, device_id=where(i), device_id_type=MESH)
    pl.semaphore_wait(barrier, n_head + Y + n_z - 3)

    def token_copy(which, i, source):
        src, dst = ((dk_ref, ok_ref), (dv_ref, ov_ref))[which]
        peer = lax.rem(head + i, n_head)
        return pltpu.make_async_remote_copy(
            src_ref=src.at[pl.ds(pl.multiple_of(peer * tokens, tokens), tokens), :],
            dst_ref=dst.at[:, pl.ds(pl.multiple_of(source * width, width), width)],
            send_sem=ssend.at[which, i], recv_sem=srecv.at[which, source],
            device_id=(me, peer), device_id_type=MESH,
        )

    def y_copy(zz, i, source):
        peer = lax.rem(y + i, Y)
        return pltpu.make_async_remote_copy(
            src_ref=dq_ref.at[zz, peer], dst_ref=ybuf.at[zz, source],
            send_sem=ysend.at[zz, i], recv_sem=yrecv.at[zz, source],
            device_id=(z * Y + peer, head), device_id_type=MESH,
        )

    def z_copy(i, source):
        peer = lax.rem(z + i, n_z)
        return pltpu.make_async_remote_copy(
            src_ref=zsend.at[peer], dst_ref=zbuf.at[source],
            send_sem=zsend_sem.at[i], recv_sem=zrecv.at[source],
            device_id=(peer * Y + y, head), device_id_type=MESH,
        )

    for i in range(1, n_z + 1):
        zz = lax.rem(z + i, n_z)
        for j in (2, 1, 3):
            y_copy(zz, j, y).start()
    for i in range(1, n_head):
        for which in range(2):
            token_copy(which, i, head).start()
    mine = []
    for which in range(2):
        src, dst = ((dk_ref, ok_ref), (dv_ref, ov_ref))[which]
        copy = pltpu.make_async_copy(
            src.at[pl.ds(pl.multiple_of(head * tokens, tokens), tokens), :],
            dst.at[:, pl.ds(pl.multiple_of(head * width, width), width)],
            own.at[which],
        )
        copy.start()
        mine.append(copy)

    for i in range(1, n_z + 1):
        zz = lax.rem(z + i, n_z)
        total = dq_ref[zz, y].astype(F32)
        for j in range(1, Y):
            source = lax.rem(y + j, Y)
            y_copy(zz, j, source).wait_recv()
            total = total + ybuf[zz, source].astype(F32)
        if i < n_z:
            zsend[zz] = total.astype(BF16)
            z_copy(i, z).start()
    for i in range(1, n_z):
        source = lax.rem(z + i, n_z)
        z_copy(i, source).wait_recv()
        total = total + zbuf[source].astype(F32)
    oq_ref[...] = total.astype(BF16)
    for copy in mine:
        copy.wait()
    for i in range(1, n_head):
        for which in range(2):
            token_copy(which, i, lax.rem(head + i, n_head)).wait_recv()
    for i in range(1, n_z + 1):
        zz = lax.rem(z + i, n_z)
        for j in range(1, Y):
            y_copy(zz, j, y).wait_send()
    for i in range(1, n_z):
        z_copy(i, z).wait_send()
    for i in range(1, n_head):
        for which in range(2):
            token_copy(which, i, head).wait_send()


def local(n_ctx, n_head, queries, prefix_keys, prefix_values, out_grad, block_lists, list_counts):
    latents, width = queries.shape
    tokens = prefix_keys.shape[0]
    heads = width // HD
    tiles = latents // TILE
    rows = heads * tiles
    n_z = n_ctx // Y
    own = latents // n_ctx
    vmem = pl.BlockSpec(memory_space=pltpu.VMEM)
    smem = pl.BlockSpec(memory_space=pltpu.SMEM)
    hbm = pl.BlockSpec(memory_space=pltpu.HBM)
    stats, table, tops, weights, dprobs = pl.pallas_call(
        functools.partial(stats_kernel, heads, tiles, 4),
        name="local_stats",
        out_shape=(
            jax.ShapeDtypeStruct((n_z, 3, GROUP, TILE), F32),
            jax.ShapeDtypeStruct((rows, 128), jnp.int32),
            jax.ShapeDtypeStruct((n_z, GROUP, TILE), F32),
            jax.ShapeDtypeStruct((rows, NEAR * BLOCK, TILE), F32),
            jax.ShapeDtypeStruct((rows, NEAR * BLOCK, TILE), F32),
        ),
        in_specs=[hbm] * 6,
        out_specs=(vmem,) * 5,
        scratch_shapes=[
            pltpu.VMEM(block_lists.shape, jnp.int32),
            pltpu.VMEM(list_counts.shape, jnp.int32),
            pltpu.VMEM(queries.shape, BF16),
            pltpu.VMEM(prefix_keys.shape, BF16),
            pltpu.VMEM(prefix_values.shape, BF16),
            pltpu.VMEM(out_grad.shape, BF16),
            pltpu.SMEM((rows, 128), jnp.int32),
            pltpu.SemaphoreType.DMA((6,)),
            pltpu.SemaphoreType.DMA,
        ],
        compiler_params=pltpu.CompilerParams(vmem_limit_bytes=VMEM_LIMIT),
    )(*[pltpu.with_memory_space_constraint(x, pltpu.HBM) for x in (block_lists, list_counts, queries, prefix_keys, prefix_values, out_grad)])
    totals = pl.pallas_call(
        functools.partial(join_kernel, n_ctx),
        name="join_stats",
        out_shape=jax.ShapeDtypeStruct((n_z, 2, GROUP, TILE), F32),
        in_specs=[vmem],
        out_specs=vmem,
        scratch_shapes=[
            pltpu.VMEM((n_z, 3, GROUP, TILE), F32),
            pltpu.VMEM((Y, 3, GROUP, TILE), F32),
            pltpu.VMEM((3, GROUP, TILE), F32),
            pltpu.VMEM((n_z, 2, GROUP, TILE), F32),
            pltpu.SemaphoreType.DMA((n_z,)),
            pltpu.SemaphoreType.DMA((n_z,)),
            pltpu.SemaphoreType.DMA((Y,)),
            pltpu.SemaphoreType.DMA((Y,)),
            pltpu.SemaphoreType.DMA((n_z,)),
            pltpu.SemaphoreType.DMA((n_z,)),
        ],
        compiler_params=pltpu.CompilerParams(collective_id=0, has_side_effects=True, vmem_limit_bytes=VMEM_LIMIT),
    )(stats)
    dq, dk, dv = pl.pallas_call(
        functools.partial(grads_kernel, heads, tiles, 4),
        name="local_grads",
        out_shape=(
            jax.ShapeDtypeStruct((latents, width), BF16),
            jax.ShapeDtypeStruct((tokens, width), BF16),
            jax.ShapeDtypeStruct((tokens, width), BF16),
        ),
        in_specs=[smem] + [vmem] * 8,
        out_specs=(vmem, vmem, vmem),
        scratch_shapes=[pltpu.VMEM((heads, tokens, 2 * HD), F32)],
        compiler_params=pltpu.CompilerParams(vmem_limit_bytes=VMEM_LIMIT),
    )(table, totals, tops, weights, dprobs, queries, prefix_keys, prefix_values, out_grad)
    piece = tokens // n_head
    results = pl.pallas_call(
        functools.partial(swap_kernel, n_ctx, n_head),
        name="swap_grads",
        out_shape=(
            jax.ShapeDtypeStruct((own, width), BF16),
            jax.ShapeDtypeStruct((piece, n_head * width), BF16),
            jax.ShapeDtypeStruct((piece, n_head * width), BF16),
        ),
        in_specs=[vmem, vmem, vmem],
        out_specs=(vmem, vmem, vmem),
        scratch_shapes=[
            pltpu.VMEM((n_z, Y, own, width), BF16),
            pltpu.VMEM((n_z, own, width), BF16),
            pltpu.VMEM((n_z, own, width), BF16),
            pltpu.SemaphoreType.DMA((2, n_head)),
            pltpu.SemaphoreType.DMA((2, n_head)),
            pltpu.SemaphoreType.DMA((n_z, Y)),
            pltpu.SemaphoreType.DMA((n_z, Y)),
            pltpu.SemaphoreType.DMA((n_z,)),
            pltpu.SemaphoreType.DMA((n_z,)),
            pltpu.SemaphoreType.DMA((2,)),
        ],
        compiler_params=pltpu.CompilerParams(collective_id=1, has_side_effects=True, vmem_limit_bytes=VMEM_LIMIT),
    )(dq.reshape(n_z, Y, own, width), dk, dv)
    return pl.pallas_call(
        functools.partial(leave_kernel, len(results)),
        name="leave",
        out_shape=tuple(jax.ShapeDtypeStruct(result.shape, result.dtype) for result in results),
        in_specs=[vmem] * len(results),
        out_specs=(hbm,) * len(results),
        scratch_shapes=[pltpu.SemaphoreType.DMA((len(results),))],
        compiler_params=pltpu.CompilerParams(vmem_limit_bytes=VMEM_LIMIT),
    )(*results)


def solution(mesh):
    return jax.shard_map(
        functools.partial(local, mesh.shape["ctx"], mesh.shape["head"]),
        mesh=mesh,
        in_specs=(
            P(None, "head"),
            P("ctx", "head"),
            P("ctx", "head"),
            P(None, "head"),
            P("head", None, None),
            P("head", None),
        ),
        out_specs=(P("ctx", "head"), P(("ctx", "head"), None), P(("ctx", "head"), None)),
        check_vma=False,
    )
```

```python
import functools

import jax
import jax.numpy as jnp
from jax import lax
from jax.experimental import pallas as pl
from jax.experimental.pallas import tpu as pltpu
from jax.sharding import PartitionSpec as P

HD = 128
TILE = 128
BLOCK = 64
MOST = 8
NEAR = 2
Y = 4
GROUP = 4
LATE = 16
LATE_AFTER = 5
MASKED = -1e30
SCALE = HD ** -0.5
SCALE2 = SCALE * 1.4426950408889634
MESH = pl.DeviceIdType.MESH
F32 = jnp.float32
BF16 = jnp.bfloat16
VMEM_LIMIT = 16 * 1024 * 1024


def dot_nt(a, b):
    return lax.dot_general(a, b, (((1,), (1,)), ((), ())), preferred_element_type=F32)


def dot_nn(a, b):
    return lax.dot_general(a, b, (((1,), (0,)), ((), ())), preferred_element_type=F32)


def dot_tn(a, b):
    return lax.dot_general(a, b, (((0,), (0,)), ((), ())), preferred_element_type=F32)


def picked(ref, table, row, head, first, slots):
    cols = pl.ds(head * HD, HD)
    parts = []
    for slot in range(first, first + slots):
        start = pl.multiple_of(table[row, slot] * BLOCK, BLOCK)
        parts.append(ref[pl.ds(start, BLOCK), cols])
    return jnp.concatenate(parts, axis=0)


def slot_table(lists, counts_row, me, blocks_here):
    tiles, sel = lists.shape
    eye = lax.broadcasted_iota(jnp.int32, (tiles, tiles), 0) == lax.broadcasted_iota(jnp.int32, (tiles, tiles), 1)
    counts = jnp.sum(jnp.where(eye, counts_row, 0), axis=1, keepdims=True)
    local = lists - me * blocks_here
    pos = lax.broadcasted_iota(jnp.int32, (tiles, sel), 1)
    listed = (pos < counts) & (local >= 0) & (local < blocks_here)
    flags = jnp.where(listed, 1.0, 0.0)
    before = lax.broadcasted_iota(jnp.int32, (sel, sel), 0) < lax.broadcasted_iota(jnp.int32, (sel, sel), 1)
    rank = dot_nn(flags.astype(BF16), jnp.where(before, 1.0, 0.0).astype(BF16))
    ids = local.astype(F32)
    lane = lax.broadcasted_iota(jnp.int32, (tiles, 128), 1)
    total = jnp.sum(flags, axis=1, keepdims=True)
    table = jnp.where(lane == MOST, total, 0.0)
    for slot in range(MOST):
        value = jnp.sum(jnp.where(listed & (rank == float(slot)), ids, 0.0), axis=1, keepdims=True)
        table = jnp.where(lane == slot, value, table)
    return table.astype(jnp.int32)


def diagonal(a, b):
    zero = jnp.zeros_like(a)
    return jnp.concatenate([jnp.concatenate([a, zero], axis=1), jnp.concatenate([zero, b], axis=1)], axis=0)


def stats_kernel(heads, tiles, unroll, lists_hbm, counts_hbm, q_hbm, k_hbm, v_hbm, g_hbm,
                 stats_ref, table_out, tops_ref, weights_ref, dprobs_ref,
                 lists_ref, counts_ref, q_ref, k_ref, v_ref, g_ref, table, sem, table_sem):
    me = lax.axis_index("ctx")
    blocks_here = k_ref.shape[0] // BLOCK
    fetches = [
        pltpu.make_async_copy(source, target, sem.at[i])
        for i, (source, target) in enumerate(
            ((lists_hbm, lists_ref), (counts_hbm, counts_ref), (k_hbm, k_ref), (q_hbm, q_ref), (v_hbm, v_ref), (g_hbm, g_ref))
        )
    ]
    for fetch in fetches:
        fetch.start()
    fetches[0].wait()
    fetches[1].wait()
    for head in range(heads):
        table_out[pl.ds(head * tiles, tiles), :] = slot_table(
            lists_ref[head], counts_ref[pl.ds(head, 1), :], me, blocks_here
        )
    copy = pltpu.make_async_copy(table_out, table, table_sem)
    copy.start()
    copy.wait()
    for fetch in fetches[2:]:
        fetch.wait()

    def part(head, tile, first, slots):
        row = head * tiles + tile
        live = (table[row, MOST] - first) * BLOCK
        rows = pl.ds(pl.multiple_of(tile * TILE, TILE), TILE)
        cols = pl.ds(head * HD, HD)
        keys = picked(k_ref, table, row, head, first, slots)
        vals = picked(v_ref, table, row, head, first, slots)
        scores = dot_nt(keys, q_ref[rows, cols]) * SCALE2
        dprobs = dot_nt(vals, g_ref[rows, cols])
        mask = lax.broadcasted_iota(jnp.int32, scores.shape, 0) < live
        scores = jnp.where(mask, scores, MASKED)
        top = jnp.max(scores, axis=0, keepdims=True)
        weights = jnp.where(mask, jnp.exp2(scores - top), 0.0)
        total = jnp.sum(weights, axis=0, keepdims=True)
        delta = jnp.sum(weights * dprobs, axis=0, keepdims=True)
        return weights, dprobs, top, total, delta

    def near(step, carry):
        for inner in range(unroll):
            for head in range(heads):
                tile = step * unroll + inner
                row = head * tiles + tile
                group = head * (tiles // GROUP) + step * (unroll // GROUP) + inner // GROUP
                place = pl.ds(inner % GROUP, 1)
                weights, dprobs, top, total, delta = part(head, tile, 0, NEAR)
                weights_ref[row] = weights
                dprobs_ref[row] = dprobs
                tops_ref[group, place, :] = top
                stats_ref[group, 0, place, :] = top
                stats_ref[group, 1, place, :] = total
                stats_ref[group, 2, place, :] = delta
        return carry

    lax.fori_loop(0, tiles // unroll, near, 0)

    def far(step, carry):
        for inner in range(GROUP):
            for head in range(heads):
                tile = step * GROUP + inner
                row = head * tiles + tile
                group = head * (tiles // GROUP) + step
                place = pl.ds(inner, 1)

                @pl.when(table[row, MOST] > NEAR)
                def _():
                    _, _, top, total, delta = part(head, tile, NEAR, MOST - NEAR)
                    old = stats_ref[group, 0, place, :]
                    joint = jnp.maximum(old, top)
                    a = jnp.exp2(old - joint)
                    b = jnp.exp2(top - joint)
                    stats_ref[group, 0, place, :] = joint
                    stats_ref[group, 1, place, :] = a * stats_ref[group, 1, place, :] + b * total
                    stats_ref[group, 2, place, :] = a * stats_ref[group, 2, place, :] + b * delta

        return carry

    lax.fori_loop(0, tiles // GROUP, far, 0)


def join_kernel(n_ctx, stats_ref, out_ref, zbuf, ybuf, part, merged, send1, recv1, send2, recv2, send3, recv3):
    me = lax.axis_index("ctx")
    head = lax.axis_index("head")
    n_z = n_ctx // Y
    z = me // Y
    y = lax.rem(me, Y)
    far_first = sorted(range(1, n_z), key=lambda i: -min(i, n_z - i))
    barrier = pltpu.get_barrier_semaphore()
    for i in far_first:
        pl.semaphore_signal(barrier, inc=1, device_id=(lax.rem(z + i, n_z) * Y + y, head), device_id_type=MESH)
    for i in range(1, Y):
        pl.semaphore_signal(barrier, inc=1, device_id=(z * Y + lax.rem(y + i, Y), head), device_id_type=MESH)
    pl.semaphore_wait(barrier, n_z + Y - 2)

    def first(i, source):
        peer = lax.rem(z + i, n_z)
        return pltpu.make_async_remote_copy(
            src_ref=stats_ref.at[peer], dst_ref=zbuf.at[source], send_sem=send1.at[i], recv_sem=recv1.at[source],
            device_id=(peer * Y + y, head), device_id_type=MESH,
        )

    def second(i, source):
        peer = lax.rem(y + i, Y)
        return pltpu.make_async_remote_copy(
            src_ref=part, dst_ref=ybuf.at[source], send_sem=send2.at[i], recv_sem=recv2.at[source],
            device_id=(z * Y + peer, head), device_id_type=MESH,
        )

    def third(i, source):
        peer = lax.rem(z + i, n_z)
        return pltpu.make_async_remote_copy(
            src_ref=merged.at[source], dst_ref=merged.at[source], send_sem=send3.at[i], recv_sem=recv3.at[source],
            device_id=(peer * Y + y, head), device_id_type=MESH,
        )

    def combine(pieces):
        tops = pieces[:, 0]
        top = jnp.max(tops, axis=0)
        share = jnp.exp2(tops - top[None])
        return top, jnp.sum(share * pieces[:, 1], axis=0), jnp.sum(share * pieces[:, 2], axis=0)

    for i in far_first:
        first(i, z).start()
    zbuf[z] = stats_ref[z]
    for i in range(1, n_z):
        first(i, lax.rem(z + i, n_z)).wait_recv()
    for kind, value in enumerate(combine(zbuf[...])):
        part[kind] = value
    for i in (2, 1, 3):
        second(i, y).start()
    ybuf[y] = part[...]
    for i in range(1, Y):
        second(i, lax.rem(y + i, Y)).wait_recv()
    top, total, delta = combine(ybuf[...])
    merged[z, 0] = top + jnp.log2(total)
    merged[z, 1] = delta / total
    for i in far_first:
        third(i, z).start()
    for i in range(1, n_z):
        first(i, z).wait_send()
    for i in range(1, Y):
        second(i, y).wait_send()
    for i in range(1, n_z):
        third(i, lax.rem(z + i, n_z)).wait_recv()
    out_ref[...] = merged[...]
    for i in range(1, n_z):
        third(i, z).wait_send()


def grads_kernel(heads, tiles, unroll, table, totals_ref, tops_ref, weights_ref, dprobs_ref, q_ref, k_ref, v_ref, g_ref,
                 dq_ref, acc):
    acc[...] = jnp.zeros_like(acc)

    def spread(head, tile, group, place, first, probs, dprobs, keys):
        row = head * tiles + tile
        rows = pl.ds(pl.multiple_of(tile * TILE, TILE), TILE)
        cols = pl.ds(head * HD, HD)
        dscores = (probs * (dprobs - totals_ref[group, 1, place, :])).astype(BF16)
        both = jnp.concatenate([dscores, probs.astype(BF16)], axis=1)
        moved = dot_nn(both, diagonal(q_ref[rows, cols], g_ref[rows, cols]))
        for slot in range(keys.shape[0] // BLOCK):
            start = pl.multiple_of(table[row, first + slot] * BLOCK, BLOCK)
            acc[head, pl.ds(start, BLOCK), :] += moved[slot * BLOCK : (slot + 1) * BLOCK]
        return dscores

    def near(step, carry):
        for inner in range(unroll):
            tile = step * unroll + inner
            rows = pl.ds(pl.multiple_of(tile * TILE, TILE), TILE)
            place = pl.ds(inner % GROUP, 1)
            pieces = []
            for head in range(heads):
                row = head * tiles + tile
                group = head * (tiles // GROUP) + step * (unroll // GROUP) + inner // GROUP
                share = jnp.exp2(tops_ref[group, place, :] - totals_ref[group, 0, place, :])
                keys = picked(k_ref, table, row, head, 0, NEAR)
                dscores = spread(head, tile, group, place, 0, weights_ref[row] * share, dprobs_ref[row], keys)
                pieces.append((dscores, keys))
            moved = dot_tn(
                jnp.concatenate([pieces[0][0], pieces[1][0]], axis=0), diagonal(pieces[0][1], pieces[1][1])
            )
            dq_ref[rows, :] = (moved * SCALE).astype(BF16)
        return carry

    lax.fori_loop(0, tiles // unroll, near, 0)

    def far(step, carry):
        for inner in range(GROUP):
            for head in range(heads):
                tile = step * GROUP + inner
                row = head * tiles + tile
                group = head * (tiles // GROUP) + step
                place = pl.ds(inner, 1)

                @pl.when(table[row, MOST] > NEAR)
                def _():
                    rows = pl.ds(pl.multiple_of(tile * TILE, TILE), TILE)
                    cols = pl.ds(head * HD, HD)
                    live = (table[row, MOST] - NEAR) * BLOCK
                    keys = picked(k_ref, table, row, head, NEAR, MOST - NEAR)
                    vals = picked(v_ref, table, row, head, NEAR, MOST - NEAR)
                    scores = dot_nt(keys, q_ref[rows, cols]) * SCALE2
                    dprobs = dot_nt(vals, g_ref[rows, cols])
                    mask = lax.broadcasted_iota(jnp.int32, scores.shape, 0) < live
                    probs = jnp.where(mask, jnp.exp2(scores - totals_ref[group, 0, place, :]), 0.0)
                    dscores = spread(head, tile, group, place, NEAR, probs, dprobs, keys)
                    extra = dot_tn(dscores, keys) * SCALE
                    dq_ref[rows, cols] = (dq_ref[rows, cols].astype(F32) + extra).astype(BF16)

        return carry

    lax.fori_loop(0, tiles // GROUP, far, 0)


def leave_kernel(count, *refs):
    sem = refs[2 * count]
    copies = [pltpu.make_async_copy(refs[i], refs[count + i], sem.at[i]) for i in range(count)]
    for copy in copies:
        copy.start()
    for copy in copies:
        copy.wait()


def swap_kernel(n_ctx, n_head, dq_ref, acc_ref, oq_ref, ok_ref, ov_ref, dk_ref, dv_ref,
                ybuf, zsend, zbuf, late_zbuf, late_send, late_ybuf,
                ssend, srecv, ysend, yrecv, zsend_sem, zrecv, late_zsend, late_zrecv, late_ysend, late_yrecv, own):
    me = lax.axis_index("ctx")
    head = lax.axis_index("head")
    n_z = n_ctx // Y
    z = me // Y
    y = lax.rem(me, Y)
    tokens = ok_ref.shape[0]
    width = dk_ref.shape[1]
    late = late_send.shape[1]
    early = oq_ref.shape[0] - late
    first_rows = pl.ds(0, early)
    last_rows = pl.ds(early, late)
    far_first = sorted(range(1, n_z), key=lambda i: -min(i, n_z - i))
    far_heads = sorted(range(1, n_head), key=lambda i: -min(i, n_head - i))
    order = far_first + [0]
    barrier = pltpu.get_barrier_semaphore()

    def at_head(i):
        return (me, lax.rem(head + i, n_head))

    def at_y(i):
        return (z * Y + lax.rem(y + i, Y), head)

    def at_z(i):
        return (lax.rem(z + i, n_z) * Y + y, head)

    for count, where in ((n_z, at_z), (n_head, at_head), (Y, at_y)):
        for i in range(1, count):
            pl.semaphore_signal(barrier, inc=1, device_id=where(i), device_id_type=MESH)
    for part in range(acc_ref.shape[0]):
        cols = pl.ds(part * HD, HD)
        dk_ref[:, cols] = (acc_ref[part, :, pl.ds(0, HD)] * SCALE).astype(BF16)
        dv_ref[:, cols] = acc_ref[part, :, pl.ds(HD, HD)].astype(BF16)
    pl.semaphore_wait(barrier, n_head + Y + n_z - 3)

    def token_copy(which, i, source):
        src, dst = ((dk_ref, ok_ref), (dv_ref, ov_ref))[which]
        peer = lax.rem(head + i, n_head)
        return pltpu.make_async_remote_copy(
            src_ref=src.at[pl.ds(pl.multiple_of(peer * tokens, tokens), tokens), :],
            dst_ref=dst.at[:, pl.ds(pl.multiple_of(source * width, width), width)],
            send_sem=ssend.at[which, i], recv_sem=srecv.at[which, source],
            device_id=(me, peer), device_id_type=MESH,
        )

    def y_copy(zz, i, source):
        peer = lax.rem(y + i, Y)
        return pltpu.make_async_remote_copy(
            src_ref=dq_ref.at[zz, peer, first_rows], dst_ref=ybuf.at[zz, source],
            send_sem=ysend.at[zz, i], recv_sem=yrecv.at[zz, source],
            device_id=(z * Y + peer, head), device_id_type=MESH,
        )

    def z_copy(i, source):
        peer = lax.rem(z + i, n_z)
        return pltpu.make_async_remote_copy(
            src_ref=zsend.at[peer], dst_ref=zbuf.at[source],
            send_sem=zsend_sem.at[i], recv_sem=zrecv.at[source],
            device_id=(peer * Y + y, head), device_id_type=MESH,
        )

    def late_z_copy(i, source):
        peer = lax.rem(z + i, n_z)
        return pltpu.make_async_remote_copy(
            src_ref=dq_ref.at[peer, :, last_rows], dst_ref=late_zbuf.at[source],
            send_sem=late_zsend.at[i], recv_sem=late_zrecv.at[source],
            device_id=(peer * Y + y, head), device_id_type=MESH,
        )

    def late_y_copy(i, source):
        peer = lax.rem(y + i, Y)
        return pltpu.make_async_remote_copy(
            src_ref=late_send.at[peer], dst_ref=late_ybuf.at[source],
            send_sem=late_ysend.at[i], recv_sem=late_yrecv.at[source],
            device_id=(z * Y + peer, head), device_id_type=MESH,
        )

    for i in far_heads:
        for which in range(2):
            token_copy(which, i, head).start()
    for i in far_first:
        late_z_copy(i, z).start()
    for i in order:
        zz = lax.rem(z + i, n_z)
        for j in (2, 1, 3):
            y_copy(zz, j, y).start()
    mine = []
    for which in range(2):
        src, dst = ((dk_ref, ok_ref), (dv_ref, ov_ref))[which]
        copy = pltpu.make_async_copy(
            src.at[pl.ds(pl.multiple_of(head * tokens, tokens), tokens), :],
            dst.at[:, pl.ds(pl.multiple_of(head * width, width), width)],
            own.at[which],
        )
        copy.start()
        mine.append(copy)

    for count, i in enumerate(order):
        zz = lax.rem(z + i, n_z)
        total = dq_ref[zz, y, first_rows].astype(F32)
        for j in range(1, Y):
            source = lax.rem(y + j, Y)
            y_copy(zz, j, source).wait_recv()
            total = total + ybuf[zz, source].astype(F32)
        if i > 0:
            zsend[zz] = total.astype(BF16)
            z_copy(i, z).start()
        if count == LATE_AFTER:
            crossed = dq_ref[z, :, last_rows].astype(F32)
            for j in range(1, n_z):
                source = lax.rem(z + j, n_z)
                late_z_copy(j, source).wait_recv()
                crossed = crossed + late_zbuf[source].astype(F32)
            late_send[...] = crossed.astype(BF16)
            for j in (2, 1, 3):
                late_y_copy(j, y).start()
    for i in range(1, n_z):
        source = lax.rem(z + i, n_z)
        z_copy(i, source).wait_recv()
        total = total + zbuf[source].astype(F32)
    oq_ref[first_rows, :] = total.astype(BF16)
    total = late_send[y].astype(F32)
    for j in range(1, Y):
        source = lax.rem(y + j, Y)
        late_y_copy(j, source).wait_recv()
        total = total + late_ybuf[source].astype(F32)
    oq_ref[last_rows, :] = total.astype(BF16)
    for copy in mine:
        copy.wait()
    for i in range(1, n_head):
        for which in range(2):
            token_copy(which, i, lax.rem(head + i, n_head)).wait_recv()
    for i in order:
        zz = lax.rem(z + i, n_z)
        for j in range(1, Y):
            y_copy(zz, j, y).wait_send()
    for i in range(1, n_z):
        z_copy(i, z).wait_send()
        late_z_copy(i, z).wait_send()
    for i in range(1, Y):
        late_y_copy(i, y).wait_send()
    for i in range(1, n_head):
        for which in range(2):
            token_copy(which, i, head).wait_send()


def local(n_ctx, n_head, queries, prefix_keys, prefix_values, out_grad, block_lists, list_counts):
    latents, width = queries.shape
    tokens = prefix_keys.shape[0]
    heads = width // HD
    tiles = latents // TILE
    rows = heads * tiles
    n_z = n_ctx // Y
    own = latents // n_ctx
    vmem = pl.BlockSpec(memory_space=pltpu.VMEM)
    smem = pl.BlockSpec(memory_space=pltpu.SMEM)
    hbm = pl.BlockSpec(memory_space=pltpu.HBM)
    stats, table, tops, weights, dprobs = pl.pallas_call(
        functools.partial(stats_kernel, heads, tiles, 4),
        name="local_stats",
        out_shape=(
            jax.ShapeDtypeStruct((n_z, 3, GROUP, TILE), F32),
            jax.ShapeDtypeStruct((rows, 128), jnp.int32),
            jax.ShapeDtypeStruct((n_z, GROUP, TILE), F32),
            jax.ShapeDtypeStruct((rows, NEAR * BLOCK, TILE), F32),
            jax.ShapeDtypeStruct((rows, NEAR * BLOCK, TILE), F32),
        ),
        in_specs=[hbm] * 6,
        out_specs=(vmem,) * 5,
        scratch_shapes=[
            pltpu.VMEM(block_lists.shape, jnp.int32),
            pltpu.VMEM(list_counts.shape, jnp.int32),
            pltpu.VMEM(queries.shape, BF16),
            pltpu.VMEM(prefix_keys.shape, BF16),
            pltpu.VMEM(prefix_values.shape, BF16),
            pltpu.VMEM(out_grad.shape, BF16),
            pltpu.SMEM((rows, 128), jnp.int32),
            pltpu.SemaphoreType.DMA((6,)),
            pltpu.SemaphoreType.DMA,
        ],
        compiler_params=pltpu.CompilerParams(vmem_limit_bytes=VMEM_LIMIT),
    )(*[pltpu.with_memory_space_constraint(x, pltpu.HBM) for x in (block_lists, list_counts, queries, prefix_keys, prefix_values, out_grad)])
    totals = pl.pallas_call(
        functools.partial(join_kernel, n_ctx),
        name="join_stats",
        out_shape=jax.ShapeDtypeStruct((n_z, 2, GROUP, TILE), F32),
        in_specs=[vmem],
        out_specs=vmem,
        scratch_shapes=[
            pltpu.VMEM((n_z, 3, GROUP, TILE), F32),
            pltpu.VMEM((Y, 3, GROUP, TILE), F32),
            pltpu.VMEM((3, GROUP, TILE), F32),
            pltpu.VMEM((n_z, 2, GROUP, TILE), F32),
            pltpu.SemaphoreType.DMA((n_z,)),
            pltpu.SemaphoreType.DMA((n_z,)),
            pltpu.SemaphoreType.DMA((Y,)),
            pltpu.SemaphoreType.DMA((Y,)),
            pltpu.SemaphoreType.DMA((n_z,)),
            pltpu.SemaphoreType.DMA((n_z,)),
        ],
        compiler_params=pltpu.CompilerParams(collective_id=0, has_side_effects=True, vmem_limit_bytes=VMEM_LIMIT),
    )(stats)
    dq, acc = pl.pallas_call(
        functools.partial(grads_kernel, heads, tiles, 4),
        name="local_grads",
        out_shape=(
            jax.ShapeDtypeStruct((latents, width), BF16),
            jax.ShapeDtypeStruct((heads, tokens, 2 * HD), F32),
        ),
        in_specs=[smem] + [vmem] * 8,
        out_specs=(vmem, vmem),
        compiler_params=pltpu.CompilerParams(vmem_limit_bytes=VMEM_LIMIT),
    )(table, totals, tops, weights, dprobs, queries, prefix_keys, prefix_values, out_grad)
    piece = tokens // n_head
    results = pl.pallas_call(
        functools.partial(swap_kernel, n_ctx, n_head),
        name="swap_grads",
        out_shape=(
            jax.ShapeDtypeStruct((own, width), BF16),
            jax.ShapeDtypeStruct((piece, n_head * width), BF16),
            jax.ShapeDtypeStruct((piece, n_head * width), BF16),
        ),
        in_specs=[vmem, vmem],
        out_specs=(vmem, vmem, vmem),
        scratch_shapes=[
            pltpu.VMEM((tokens, width), BF16),
            pltpu.VMEM((tokens, width), BF16),
            pltpu.VMEM((n_z, Y, own - LATE, width), BF16),
            pltpu.VMEM((n_z, own - LATE, width), BF16),
            pltpu.VMEM((n_z, own - LATE, width), BF16),
            pltpu.VMEM((n_z, Y, LATE, width), BF16),
            pltpu.VMEM((Y, LATE, width), BF16),
            pltpu.VMEM((Y, LATE, width), BF16),
            pltpu.SemaphoreType.DMA((2, n_head)),
            pltpu.SemaphoreType.DMA((2, n_head)),
            pltpu.SemaphoreType.DMA((n_z, Y)),
            pltpu.SemaphoreType.DMA((n_z, Y)),
            pltpu.SemaphoreType.DMA((n_z,)),
            pltpu.SemaphoreType.DMA((n_z,)),
            pltpu.SemaphoreType.DMA((n_z,)),
            pltpu.SemaphoreType.DMA((n_z,)),
            pltpu.SemaphoreType.DMA((Y,)),
            pltpu.SemaphoreType.DMA((Y,)),
            pltpu.SemaphoreType.DMA((2,)),
        ],
        compiler_params=pltpu.CompilerParams(collective_id=1, has_side_effects=True, vmem_limit_bytes=VMEM_LIMIT),
    )(dq.reshape(n_z, Y, own, width), acc)
    return pl.pallas_call(
        functools.partial(leave_kernel, len(results)),
        name="leave",
        out_shape=tuple(jax.ShapeDtypeStruct(result.shape, result.dtype) for result in results),
        in_specs=[vmem] * len(results),
        out_specs=(hbm,) * len(results),
        scratch_shapes=[pltpu.SemaphoreType.DMA((len(results),))],
        compiler_params=pltpu.CompilerParams(vmem_limit_bytes=VMEM_LIMIT),
    )(*results)


def solution(mesh):
    return jax.shard_map(
        functools.partial(local, mesh.shape["ctx"], mesh.shape["head"]),
        mesh=mesh,
        in_specs=(
            P(None, "head"),
            P("ctx", "head"),
            P("ctx", "head"),
            P(None, "head"),
            P("head", None, None),
            P("head", None),
        ),
        out_specs=(P("ctx", "head"), P(("ctx", "head"), None), P(("ctx", "head"), None)),
        check_vma=False,
    )
```

```python
import functools

import jax
import jax.numpy as jnp
from jax import lax
from jax.experimental import pallas as pl
from jax.experimental.pallas import tpu as pltpu
from jax.sharding import PartitionSpec as P

HD = 128
TILE = 128
BLOCK = 64
MOST = 8
NEAR = 2
Y = 4
GROUP = 4
LATE = 16
UNROLL = 16
QUEUE = MOST + 1
LENGTH = MOST + 2
LATE_AFTER = 5
MASKED = -1e30
SCALE = HD ** -0.5
SCALE2 = SCALE * 1.4426950408889634
MESH = pl.DeviceIdType.MESH
F32 = jnp.float32
BF16 = jnp.bfloat16
VMEM_LIMIT = 32 * 1024 * 1024


def dot_nt(a, b):
    return lax.dot_general(a, b, (((1,), (1,)), ((), ())), preferred_element_type=F32)


def dot_nn(a, b):
    return lax.dot_general(a, b, (((1,), (0,)), ((), ())), preferred_element_type=F32)


def dot_tn(a, b):
    return lax.dot_general(a, b, (((0,), (0,)), ((), ())), preferred_element_type=F32)


def span(index, size):
    start = index * size
    return pl.ds(start if isinstance(start, int) else pl.multiple_of(start, size), size)


def picked(ref, table, row, head, first, slots):
    cols = span(head, HD)
    return jnp.concatenate([ref[table[row, slot], :, cols] for slot in range(first, first + slots)], axis=0)


def slot_table(lists, counts_rows, me, blocks_here):
    heads, tiles, sel = lists.shape
    rows = heads * tiles
    eye = lax.broadcasted_iota(jnp.int32, (tiles, tiles), 0) == lax.broadcasted_iota(jnp.int32, (tiles, tiles), 1)
    counts = jnp.concatenate(
        [jnp.sum(jnp.where(eye, counts_rows[head : head + 1], 0), axis=1, keepdims=True) for head in range(heads)], axis=0
    )
    local = lists.reshape(rows, sel) - me * blocks_here
    pos = lax.broadcasted_iota(jnp.int32, (rows, sel), 1)
    listed = (pos < counts) & (local >= 0) & (local < blocks_here)
    flags = jnp.where(listed, 1.0, 0.0)
    before = lax.broadcasted_iota(jnp.int32, (sel, sel), 0) < lax.broadcasted_iota(jnp.int32, (sel, sel), 1)
    rank = dot_nn(flags.astype(BF16), jnp.where(before, 1.0, 0.0).astype(BF16))
    ids = local.astype(F32)
    lane = lax.broadcasted_iota(jnp.int32, (rows, 128), 1)
    total = jnp.sum(flags, axis=1, keepdims=True)
    more = jnp.where(total > float(NEAR), 1.0, 0.0)
    row = lax.broadcasted_iota(jnp.int32, (rows, 128), 0)
    above = lax.broadcasted_iota(jnp.int32, (rows, rows), 1) < lax.broadcasted_iota(jnp.int32, (rows, rows), 0)
    wide = jnp.broadcast_to(more, (rows, 128))
    order = dot_nn(jnp.where(above, 1.0, 0.0).astype(BF16), wide.astype(BF16))
    chosen = jnp.where((order == lane.astype(F32)) & (wide > 0.0), 1.0, 0.0)
    queue = dot_tn(chosen.astype(BF16), row.astype(F32).astype(BF16))[:rows]
    table = jnp.where(lane == MOST, total, 0.0)
    for slot in range(MOST):
        value = jnp.sum(jnp.where(listed & (rank == float(slot)), ids, 0.0), axis=1, keepdims=True)
        table = jnp.where(lane == slot, value, table)
    table = jnp.where(lane == QUEUE, queue, table)
    table = jnp.where(lane == LENGTH, jnp.sum(wide, axis=0, keepdims=True), table)
    return table.astype(jnp.int32)


def diagonal(a, b):
    zero = jnp.zeros_like(a)
    return jnp.concatenate([jnp.concatenate([a, zero], axis=1), jnp.concatenate([zero, b], axis=1)], axis=0)


def slot_stats(heads, tiles, table, q_ref, k_ref, v_ref, g_ref, head, tile, first, slots):
    row = head * tiles + tile
    live = (table[row, MOST] - first) * BLOCK
    rows = span(tile, TILE)
    cols = span(head, HD)
    keys = picked(k_ref, table, row, head, first, slots)
    vals = picked(v_ref, table, row, head, first, slots)
    scores = dot_nt(keys, q_ref[rows, cols]) * SCALE2
    dprobs = dot_nt(vals, g_ref[rows, cols])
    mask = lax.broadcasted_iota(jnp.int32, scores.shape, 0) < live
    scores = jnp.where(mask, scores, MASKED)
    top = jnp.max(scores, axis=0, keepdims=True)
    weights = jnp.where(mask, jnp.exp2(scores - top), 0.0)
    total = jnp.sum(weights, axis=0, keepdims=True)
    delta = jnp.sum(weights * dprobs, axis=0, keepdims=True)
    return weights, dprobs, top, total, delta


def fetch_kernel(heads, tiles, lists_hbm, counts_hbm, q_hbm, k_hbm, v_hbm, g_hbm,
                 stats_ref, table_out, far_tops_ref, far_weights_ref, far_dprobs_ref, q_ref, k_ref, v_ref, g_ref,
                 lists_ref, counts_ref, table, sem, table_sem):
    me = lax.axis_index("ctx")
    blocks_here = k_ref.shape[0]
    pieces = [
        (lists_hbm, lists_ref), (counts_hbm, counts_ref),
        (k_hbm, k_ref), (v_hbm, v_ref), (q_hbm, q_ref), (g_hbm, g_ref),
    ]
    fetches = [pltpu.make_async_copy(source, target, sem.at[i]) for i, (source, target) in enumerate(pieces)]
    for fetch in fetches:
        fetch.start()
    stats_ref[:, 0] = jnp.full_like(stats_ref[:, 0], MASKED)
    stats_ref[:, 1] = jnp.zeros_like(stats_ref[:, 1])
    stats_ref[:, 2] = jnp.zeros_like(stats_ref[:, 2])
    fetches[0].wait()
    fetches[1].wait()
    table_out[...] = slot_table(lists_ref[...], counts_ref[...], me, blocks_here)
    copy = pltpu.make_async_copy(table_out, table, table_sem)
    copy.start()
    copy.wait()
    for fetch in fetches[2:]:
        fetch.wait()

    def far(item, carry):
        row = table[item, QUEUE]
        group = row // GROUP
        place = pl.ds(lax.rem(row, GROUP), 1)
        weights, dprobs, top, total, delta = slot_stats(
            heads, tiles, table, q_ref, k_ref, v_ref, g_ref, row // tiles, lax.rem(row, tiles), NEAR, MOST - NEAR
        )
        far_weights_ref[item] = weights
        far_dprobs_ref[item] = dprobs
        far_tops_ref[item] = top
        stats_ref[group, 0, place, :] = top
        stats_ref[group, 1, place, :] = total
        stats_ref[group, 2, place, :] = delta
        return carry

    lax.fori_loop(0, table[0, LENGTH], far, 0)


def join_kernel(n_ctx, heads, tiles, unroll, table, far_ref, q_ref, k_ref, v_ref, g_ref,
                out_ref, tops_ref, weights_ref, dprobs_ref, stats_ref, zbuf, ybuf, part, merged, send1, recv1, send2, recv2, send3, recv3):
    me = lax.axis_index("ctx")
    head = lax.axis_index("head")
    n_z = n_ctx // Y
    z = me // Y
    y = lax.rem(me, Y)
    far_first = sorted(range(1, n_z), key=lambda i: -min(i, n_z - i))
    barrier = pltpu.get_barrier_semaphore()
    for i in far_first:
        pl.semaphore_signal(barrier, inc=1, device_id=(lax.rem(z + i, n_z) * Y + y, head), device_id_type=MESH)
    for i in range(1, Y):
        pl.semaphore_signal(barrier, inc=1, device_id=(z * Y + lax.rem(y + i, Y), head), device_id_type=MESH)

    def near(step, carry):
        for inner in range(unroll):
            for part_head in range(heads):
                tile = step * unroll + inner
                row = part_head * tiles + tile
                group = part_head * (tiles // GROUP) + step * (unroll // GROUP) + inner // GROUP
                place = pl.ds(inner % GROUP, 1)
                weights, dprobs, top, total, delta = slot_stats(
                    heads, tiles, table, q_ref, k_ref, v_ref, g_ref, part_head, tile, 0, NEAR
                )
                weights_ref[row] = weights
                dprobs_ref[row] = dprobs
                tops_ref[group, place, :] = top
                stats_ref[group, 1, place, :] = total
                stats_ref[group, 2, place, :] = delta
        return carry

    lax.fori_loop(0, tiles // unroll, near, 0)
    tops = tops_ref[...]
    joint = jnp.maximum(tops, far_ref[:, 0])
    here = jnp.exp2(tops - joint)
    there = jnp.exp2(far_ref[:, 0] - joint)
    stats_ref[:, 0] = joint
    for kind in (1, 2):
        stats_ref[:, kind] = here * stats_ref[:, kind] + there * far_ref[:, kind]
    pl.semaphore_wait(barrier, n_z + Y - 2)

    def first(i, source):
        peer = lax.rem(z + i, n_z)
        return pltpu.make_async_remote_copy(
            src_ref=stats_ref.at[peer], dst_ref=zbuf.at[source], send_sem=send1.at[i], recv_sem=recv1.at[source],
            device_id=(peer * Y + y, head), device_id_type=MESH,
        )

    def second(i, source):
        peer = lax.rem(y + i, Y)
        return pltpu.make_async_remote_copy(
            src_ref=part, dst_ref=ybuf.at[source], send_sem=send2.at[i], recv_sem=recv2.at[source],
            device_id=(z * Y + peer, head), device_id_type=MESH,
        )

    def third(i, source):
        peer = lax.rem(z + i, n_z)
        return pltpu.make_async_remote_copy(
            src_ref=merged.at[source], dst_ref=merged.at[source], send_sem=send3.at[i], recv_sem=recv3.at[source],
            device_id=(peer * Y + y, head), device_id_type=MESH,
        )

    def combine(pieces):
        tops = pieces[:, 0]
        top = jnp.max(tops, axis=0)
        share = jnp.exp2(tops - top[None])
        return top, jnp.sum(share * pieces[:, 1], axis=0), jnp.sum(share * pieces[:, 2], axis=0)

    for i in far_first:
        first(i, z).start()
    zbuf[z] = stats_ref[z]
    for i in range(1, n_z):
        first(i, lax.rem(z + i, n_z)).wait_recv()
    for kind, value in enumerate(combine(zbuf[...])):
        part[kind] = value
    for i in (2, 1, 3):
        second(i, y).start()
    ybuf[y] = part[...]
    for i in range(1, Y):
        second(i, lax.rem(y + i, Y)).wait_recv()
    top, total, delta = combine(ybuf[...])
    merged[z, 0] = top + jnp.log2(total)
    merged[z, 1] = delta / total
    for i in far_first:
        third(i, z).start()
    for i in range(1, n_z):
        first(i, z).wait_send()
    for i in range(1, Y):
        second(i, y).wait_send()
    for i in range(1, n_z):
        third(i, lax.rem(z + i, n_z)).wait_recv()
    out_ref[...] = merged[...]
    for i in range(1, n_z):
        third(i, z).wait_send()


def grads_kernel(heads, tiles, unroll, table, totals_ref, tops_ref, weights_ref, dprobs_ref,
                 far_tops_ref, far_weights_ref, far_dprobs_ref, q_ref, k_ref, g_ref, dq_ref, acc):
    acc[...] = jnp.zeros_like(acc)

    def spread(head, tile, group, place, first, probs, dprobs, keys):
        row = head * tiles + tile
        rows = span(tile, TILE)
        cols = span(head, HD)
        dscores = (probs * (dprobs - totals_ref[group, 1, place, :])).astype(BF16)
        both = jnp.concatenate([dscores, probs.astype(BF16)], axis=1)
        moved = dot_nn(both, diagonal(q_ref[rows, cols], g_ref[rows, cols]))
        for slot in range(keys.shape[0] // BLOCK):
            start = pl.multiple_of(table[row, first + slot] * BLOCK, BLOCK)
            acc[head, pl.ds(start, BLOCK), :] += moved[slot * BLOCK : (slot + 1) * BLOCK]
        return dscores

    for step in range(tiles // unroll):
        for inner in range(unroll):
            tile = step * unroll + inner
            rows = span(tile, TILE)
            place = pl.ds(inner % GROUP, 1)
            pieces = []
            for head in range(heads):
                row = head * tiles + tile
                group = head * (tiles // GROUP) + step * (unroll // GROUP) + inner // GROUP
                share = jnp.exp2(tops_ref[group, place, :] - totals_ref[group, 0, place, :])
                keys = picked(k_ref, table, row, head, 0, NEAR)
                dscores = spread(head, tile, group, place, 0, weights_ref[row] * share, dprobs_ref[row], keys)
                pieces.append((dscores, keys))
            moved = dot_tn(
                jnp.concatenate([pieces[0][0], pieces[1][0]], axis=0), diagonal(pieces[0][1], pieces[1][1])
            )
            dq_ref[rows, :] = (moved * SCALE).astype(BF16)

    def far(item, carry):
        row = table[item, QUEUE]
        head = row // tiles
        tile = lax.rem(row, tiles)
        group = row // GROUP
        place = pl.ds(lax.rem(row, GROUP), 1)
        rows = span(tile, TILE)
        cols = span(head, HD)
        share = jnp.exp2(far_tops_ref[item] - totals_ref[group, 0, place, :])
        keys = picked(k_ref, table, row, head, NEAR, MOST - NEAR)
        dscores = spread(head, tile, group, place, NEAR, far_weights_ref[item] * share, far_dprobs_ref[item], keys)
        extra = dot_tn(dscores, keys) * SCALE
        dq_ref[rows, cols] = (dq_ref[rows, cols].astype(F32) + extra).astype(BF16)
        return carry

    lax.fori_loop(0, table[0, LENGTH], far, 0)


def leave_kernel(count, *refs):
    sem = refs[2 * count]
    copies = [pltpu.make_async_copy(refs[i], refs[count + i], sem.at[i]) for i in range(count)]
    for copy in copies:
        copy.start()
    for copy in copies:
        copy.wait()


def swap_kernel(n_ctx, n_head, dq_ref, acc_ref, oq_ref, ok_ref, ov_ref, dk_ref, dv_ref,
                ybuf, zsend, zbuf, late_zbuf, late_send, late_ybuf,
                ssend, srecv, ysend, yrecv, zsend_sem, zrecv, late_zsend, late_zrecv, late_ysend, late_yrecv, own):
    me = lax.axis_index("ctx")
    head = lax.axis_index("head")
    n_z = n_ctx // Y
    z = me // Y
    y = lax.rem(me, Y)
    tokens = ok_ref.shape[0]
    width = dk_ref.shape[1]
    late = late_send.shape[1]
    early = oq_ref.shape[0] - late
    first_rows = pl.ds(0, early)
    last_rows = pl.ds(early, late)
    far_first = sorted(range(1, n_z), key=lambda i: -min(i, n_z - i))
    far_heads = sorted(range(1, n_head), key=lambda i: -min(i, n_head - i))
    order = far_first + [0]
    barrier = pltpu.get_barrier_semaphore()

    def at_head(i):
        return (me, lax.rem(head + i, n_head))

    def at_y(i):
        return (z * Y + lax.rem(y + i, Y), head)

    def at_z(i):
        return (lax.rem(z + i, n_z) * Y + y, head)

    for count, where in ((n_z, at_z), (n_head, at_head), (Y, at_y)):
        for i in range(1, count):
            pl.semaphore_signal(barrier, inc=1, device_id=where(i), device_id_type=MESH)
    for part in range(acc_ref.shape[0]):
        cols = pl.ds(part * HD, HD)
        dk_ref[:, cols] = (acc_ref[part, :, pl.ds(0, HD)] * SCALE).astype(BF16)
        dv_ref[:, cols] = acc_ref[part, :, pl.ds(HD, HD)].astype(BF16)
    pl.semaphore_wait(barrier, n_head + Y + n_z - 3)

    def token_copy(which, i, source):
        src, dst = ((dk_ref, ok_ref), (dv_ref, ov_ref))[which]
        peer = lax.rem(head + i, n_head)
        return pltpu.make_async_remote_copy(
            src_ref=src.at[pl.ds(pl.multiple_of(peer * tokens, tokens), tokens), :],
            dst_ref=dst.at[:, pl.ds(pl.multiple_of(source * width, width), width)],
            send_sem=ssend.at[which, i], recv_sem=srecv.at[which, source],
            device_id=(me, peer), device_id_type=MESH,
        )

    def y_copy(zz, i, source):
        peer = lax.rem(y + i, Y)
        return pltpu.make_async_remote_copy(
            src_ref=dq_ref.at[zz, peer, first_rows], dst_ref=ybuf.at[zz, source],
            send_sem=ysend.at[zz, i], recv_sem=yrecv.at[zz, source],
            device_id=(z * Y + peer, head), device_id_type=MESH,
        )

    def z_copy(i, source):
        peer = lax.rem(z + i, n_z)
        return pltpu.make_async_remote_copy(
            src_ref=zsend.at[peer], dst_ref=zbuf.at[source],
            send_sem=zsend_sem.at[i], recv_sem=zrecv.at[source],
            device_id=(peer * Y + y, head), device_id_type=MESH,
        )

    def late_z_copy(i, source):
        peer = lax.rem(z + i, n_z)
        return pltpu.make_async_remote_copy(
            src_ref=dq_ref.at[peer, :, last_rows], dst_ref=late_zbuf.at[source],
            send_sem=late_zsend.at[i], recv_sem=late_zrecv.at[source],
            device_id=(peer * Y + y, head), device_id_type=MESH,
        )

    def late_y_copy(i, source):
        peer = lax.rem(y + i, Y)
        return pltpu.make_async_remote_copy(
            src_ref=late_send.at[peer], dst_ref=late_ybuf.at[source],
            send_sem=late_ysend.at[i], recv_sem=late_yrecv.at[source],
            device_id=(z * Y + peer, head), device_id_type=MESH,
        )

    for i in far_heads:
        for which in range(2):
            token_copy(which, i, head).start()
    for i in far_first:
        late_z_copy(i, z).start()
    for i in order:
        zz = lax.rem(z + i, n_z)
        for j in (2, 1, 3):
            y_copy(zz, j, y).start()
    mine = []
    for which in range(2):
        src, dst = ((dk_ref, ok_ref), (dv_ref, ov_ref))[which]
        copy = pltpu.make_async_copy(
            src.at[pl.ds(pl.multiple_of(head * tokens, tokens), tokens), :],
            dst.at[:, pl.ds(pl.multiple_of(head * width, width), width)],
            own.at[which],
        )
        copy.start()
        mine.append(copy)

    for count, i in enumerate(order):
        zz = lax.rem(z + i, n_z)
        total = dq_ref[zz, y, first_rows].astype(F32)
        for j in range(1, Y):
            source = lax.rem(y + j, Y)
            y_copy(zz, j, source).wait_recv()
            total = total + ybuf[zz, source].astype(F32)
        if i > 0:
            zsend[zz] = total.astype(BF16)
            z_copy(i, z).start()
        if count == LATE_AFTER:
            crossed = dq_ref[z, :, last_rows].astype(F32)
            for j in range(1, n_z):
                source = lax.rem(z + j, n_z)
                late_z_copy(j, source).wait_recv()
                crossed = crossed + late_zbuf[source].astype(F32)
            late_send[...] = crossed.astype(BF16)
            for j in (2, 1, 3):
                late_y_copy(j, y).start()
    for i in range(1, n_z):
        source = lax.rem(z + i, n_z)
        z_copy(i, source).wait_recv()
        total = total + zbuf[source].astype(F32)
    oq_ref[first_rows, :] = total.astype(BF16)
    total = late_send[y].astype(F32)
    for j in range(1, Y):
        source = lax.rem(y + j, Y)
        late_y_copy(j, source).wait_recv()
        total = total + late_ybuf[source].astype(F32)
    oq_ref[last_rows, :] = total.astype(BF16)
    for copy in mine:
        copy.wait()
    for i in range(1, n_head):
        for which in range(2):
            token_copy(which, i, lax.rem(head + i, n_head)).wait_recv()
    for i in order:
        zz = lax.rem(z + i, n_z)
        for j in range(1, Y):
            y_copy(zz, j, y).wait_send()
    for i in range(1, n_z):
        z_copy(i, z).wait_send()
        late_z_copy(i, z).wait_send()
    for i in range(1, Y):
        late_y_copy(i, y).wait_send()
    for i in range(1, n_head):
        for which in range(2):
            token_copy(which, i, head).wait_send()


def local(n_ctx, n_head, queries, prefix_keys, prefix_values, out_grad, block_lists, list_counts):
    latents, width = queries.shape
    tokens = prefix_keys.shape[0]
    heads = width // HD
    tiles = latents // TILE
    rows = heads * tiles
    n_z = n_ctx // Y
    own = latents // n_ctx
    vmem = pl.BlockSpec(memory_space=pltpu.VMEM)
    smem = pl.BlockSpec(memory_space=pltpu.SMEM)
    hbm = pl.BlockSpec(memory_space=pltpu.HBM)
    prefix_keys = prefix_keys.reshape(tokens // BLOCK, BLOCK, width)
    prefix_values = prefix_values.reshape(tokens // BLOCK, BLOCK, width)
    operands = (block_lists, list_counts, queries, prefix_keys, prefix_values, out_grad)
    far_shape = (rows, (MOST - NEAR) * BLOCK, TILE)
    near_shape = (rows, NEAR * BLOCK, TILE)
    far_stats, table, *far_kept, queries, prefix_keys, prefix_values, out_grad = pl.pallas_call(
        functools.partial(fetch_kernel, heads, tiles),
        name="fetch",
        out_shape=(
            jax.ShapeDtypeStruct((n_z, 3, GROUP, TILE), F32),
            jax.ShapeDtypeStruct((rows, 128), jnp.int32),
            jax.ShapeDtypeStruct((rows, 1, TILE), F32),
            jax.ShapeDtypeStruct(far_shape, F32),
            jax.ShapeDtypeStruct(far_shape, F32),
            jax.ShapeDtypeStruct(queries.shape, BF16),
            jax.ShapeDtypeStruct(prefix_keys.shape, BF16),
            jax.ShapeDtypeStruct(prefix_values.shape, BF16),
            jax.ShapeDtypeStruct(out_grad.shape, BF16),
        ),
        in_specs=[hbm] * 6,
        out_specs=(vmem,) * 9,
        scratch_shapes=[
            pltpu.VMEM(block_lists.shape, jnp.int32),
            pltpu.VMEM(list_counts.shape, jnp.int32),
            pltpu.SMEM((rows, 128), jnp.int32),
            pltpu.SemaphoreType.DMA((6,)),
            pltpu.SemaphoreType.DMA,
        ],
        compiler_params=pltpu.CompilerParams(vmem_limit_bytes=VMEM_LIMIT),
    )(*[pltpu.with_memory_space_constraint(x, pltpu.HBM) for x in operands])
    totals, *near_kept = pl.pallas_call(
        functools.partial(join_kernel, n_ctx, heads, tiles, 8),
        name="join_stats",
        out_shape=(
            jax.ShapeDtypeStruct((n_z, 2, GROUP, TILE), F32),
            jax.ShapeDtypeStruct((n_z, GROUP, TILE), F32),
            jax.ShapeDtypeStruct(near_shape, F32),
            jax.ShapeDtypeStruct(near_shape, F32),
        ),
        in_specs=[smem] + [vmem] * 5,
        out_specs=(vmem,) * 4,
        scratch_shapes=[
            pltpu.VMEM((n_z, 3, GROUP, TILE), F32),
            pltpu.VMEM((n_z, 3, GROUP, TILE), F32),
            pltpu.VMEM((Y, 3, GROUP, TILE), F32),
            pltpu.VMEM((3, GROUP, TILE), F32),
            pltpu.VMEM((n_z, 2, GROUP, TILE), F32),
            pltpu.SemaphoreType.DMA((n_z,)),
            pltpu.SemaphoreType.DMA((n_z,)),
            pltpu.SemaphoreType.DMA((Y,)),
            pltpu.SemaphoreType.DMA((Y,)),
            pltpu.SemaphoreType.DMA((n_z,)),
            pltpu.SemaphoreType.DMA((n_z,)),
        ],
        compiler_params=pltpu.CompilerParams(collective_id=0, has_side_effects=True, vmem_limit_bytes=VMEM_LIMIT // 2),
    )(table, far_stats, queries, prefix_keys, prefix_values, out_grad)
    dq, acc = pl.pallas_call(
        functools.partial(grads_kernel, heads, tiles, 4),
        name="local_grads",
        out_shape=(
            jax.ShapeDtypeStruct((latents, width), BF16),
            jax.ShapeDtypeStruct((heads, tokens, 2 * HD), F32),
        ),
        in_specs=[smem] + [vmem] * 10,
        out_specs=(vmem, vmem),
        compiler_params=pltpu.CompilerParams(vmem_limit_bytes=VMEM_LIMIT),
    )(table, totals, *near_kept, *far_kept, queries, prefix_keys, out_grad)
    piece = tokens // n_head
    results = pl.pallas_call(
        functools.partial(swap_kernel, n_ctx, n_head),
        name="swap_grads",
        out_shape=(
            jax.ShapeDtypeStruct((own, width), BF16),
            jax.ShapeDtypeStruct((piece, n_head * width), BF16),
            jax.ShapeDtypeStruct((piece, n_head * width), BF16),
        ),
        in_specs=[vmem, vmem],
        out_specs=(vmem, vmem, vmem),
        scratch_shapes=[
            pltpu.VMEM((tokens, width), BF16),
            pltpu.VMEM((tokens, width), BF16),
            pltpu.VMEM((n_z, Y, own - LATE, width), BF16),
            pltpu.VMEM((n_z, own - LATE, width), BF16),
            pltpu.VMEM((n_z, own - LATE, width), BF16),
            pltpu.VMEM((n_z, Y, LATE, width), BF16),
            pltpu.VMEM((Y, LATE, width), BF16),
            pltpu.VMEM((Y, LATE, width), BF16),
            pltpu.SemaphoreType.DMA((2, n_head)),
            pltpu.SemaphoreType.DMA((2, n_head)),
            pltpu.SemaphoreType.DMA((n_z, Y)),
            pltpu.SemaphoreType.DMA((n_z, Y)),
            pltpu.SemaphoreType.DMA((n_z,)),
            pltpu.SemaphoreType.DMA((n_z,)),
            pltpu.SemaphoreType.DMA((n_z,)),
            pltpu.SemaphoreType.DMA((n_z,)),
            pltpu.SemaphoreType.DMA((Y,)),
            pltpu.SemaphoreType.DMA((Y,)),
            pltpu.SemaphoreType.DMA((2,)),
        ],
        compiler_params=pltpu.CompilerParams(collective_id=1, has_side_effects=True, vmem_limit_bytes=VMEM_LIMIT // 2),
    )(dq.reshape(n_z, Y, own, width), acc)
    return pl.pallas_call(
        functools.partial(leave_kernel, len(results)),
        name="leave",
        out_shape=tuple(jax.ShapeDtypeStruct(result.shape, result.dtype) for result in results),
        in_specs=[vmem] * len(results),
        out_specs=(hbm,) * len(results),
        scratch_shapes=[pltpu.SemaphoreType.DMA((len(results),))],
        compiler_params=pltpu.CompilerParams(vmem_limit_bytes=VMEM_LIMIT),
    )(*results)


def solution(mesh):
    return jax.shard_map(
        functools.partial(local, mesh.shape["ctx"], mesh.shape["head"]),
        mesh=mesh,
        in_specs=(
            P(None, "head"),
            P("ctx", "head"),
            P("ctx", "head"),
            P(None, "head"),
            P("head", None, None),
            P("head", None),
        ),
        out_specs=(P("ctx", "head"), P(("ctx", "head"), None), P(("ctx", "head"), None)),
        check_vma=False,
    )
```

```python
import functools

import jax
import jax.numpy as jnp
from jax import lax
from jax.experimental import pallas as pl
from jax.experimental.pallas import tpu as pltpu
from jax.sharding import PartitionSpec as P

HD = 128
TILE = 128
BLOCK = 64
MOST = 8
NEAR = 2
Y = 4
GROUP = 4
PAIR = 2
LATE = 16
UNROLL = 16
QUEUE = MOST + 1
LENGTH = MOST + 2
LATE_AFTER = 5
MASKED = -1e30
SCALE = HD ** -0.5
SCALE2 = SCALE * 1.4426950408889634
MESH = pl.DeviceIdType.MESH
F32 = jnp.float32
BF16 = jnp.bfloat16
VMEM_LIMIT = 32 * 1024 * 1024


def dot_nt(a, b):
    return lax.dot_general(a, b, (((1,), (1,)), ((), ())), preferred_element_type=F32)


def dot_nn(a, b):
    return lax.dot_general(a, b, (((1,), (0,)), ((), ())), preferred_element_type=F32)


def dot_tn(a, b):
    return lax.dot_general(a, b, (((0,), (0,)), ((), ())), preferred_element_type=F32)


def span(index, size):
    start = index * size
    return pl.ds(start if isinstance(start, int) else pl.multiple_of(start, size), size)


def picked(ref, table, row, head, first, slots):
    cols = span(head, HD)
    return jnp.concatenate([ref[table[row, slot], :, cols] for slot in range(first, first + slots)], axis=0)


def slot_table(lists, counts_rows, me, blocks_here):
    heads, tiles, sel = lists.shape
    rows = heads * tiles
    eye = lax.broadcasted_iota(jnp.int32, (tiles, tiles), 0) == lax.broadcasted_iota(jnp.int32, (tiles, tiles), 1)
    counts = jnp.concatenate(
        [jnp.sum(jnp.where(eye, counts_rows[head : head + 1], 0), axis=1, keepdims=True) for head in range(heads)], axis=0
    )
    local = lists.reshape(rows, sel) - me * blocks_here
    pos = lax.broadcasted_iota(jnp.int32, (rows, sel), 1)
    listed = (pos < counts) & (local >= 0) & (local < blocks_here)
    flags = jnp.where(listed, 1.0, 0.0)
    before = lax.broadcasted_iota(jnp.int32, (sel, sel), 0) < lax.broadcasted_iota(jnp.int32, (sel, sel), 1)
    rank = dot_nn(flags.astype(BF16), jnp.where(before, 1.0, 0.0).astype(BF16))
    ids = local.astype(F32)
    lane = lax.broadcasted_iota(jnp.int32, (rows, 128), 1)
    total = jnp.sum(flags, axis=1, keepdims=True)
    more = jnp.where(total > float(NEAR), 1.0, 0.0)
    row = lax.broadcasted_iota(jnp.int32, (rows, 128), 0)
    above = lax.broadcasted_iota(jnp.int32, (rows, rows), 1) < lax.broadcasted_iota(jnp.int32, (rows, rows), 0)
    wide = jnp.broadcast_to(more, (rows, 128))
    order = dot_nn(jnp.where(above, 1.0, 0.0).astype(BF16), wide.astype(BF16))
    chosen = jnp.where((order == lane.astype(F32)) & (wide > 0.0), 1.0, 0.0)
    queue = dot_tn(chosen.astype(BF16), row.astype(F32).astype(BF16))[:rows]
    table = jnp.where(lane == MOST, total, 0.0)
    for slot in range(MOST):
        value = jnp.sum(jnp.where(listed & (rank == float(slot)), ids, 0.0), axis=1, keepdims=True)
        table = jnp.where(lane == slot, value, table)
    table = jnp.where(lane == QUEUE, queue, table)
    table = jnp.where(lane == LENGTH, jnp.sum(wide, axis=0, keepdims=True), table)
    return table.astype(jnp.int32)


def diagonal(a, b):
    zero = jnp.zeros_like(a)
    return jnp.concatenate([jnp.concatenate([a, zero], axis=1), jnp.concatenate([zero, b], axis=1)], axis=0)


def seat(head, tile):
    inner = tile % PAIR if isinstance(tile, int) else lax.rem(tile, PAIR)
    return tile // PAIR, pl.ds(head * PAIR + inner, 1)


def slot_stats(heads, tiles, table, q_ref, k_ref, v_ref, g_ref, head, tile, first, slots):
    row = head * tiles + tile
    live = (table[row, MOST] - first) * BLOCK
    rows = span(tile, TILE)
    cols = span(head, HD)
    keys = picked(k_ref, table, row, head, first, slots)
    vals = picked(v_ref, table, row, head, first, slots)
    scores = dot_nt(keys, q_ref[rows, cols]) * SCALE2
    dprobs = dot_nt(vals, g_ref[rows, cols])
    mask = lax.broadcasted_iota(jnp.int32, scores.shape, 0) < live
    scores = jnp.where(mask, scores, MASKED)
    top = jnp.max(scores, axis=0, keepdims=True)
    weights = jnp.where(mask, jnp.exp2(scores - top), 0.0)
    total = jnp.sum(weights, axis=0, keepdims=True)
    delta = jnp.sum(weights * dprobs, axis=0, keepdims=True)
    return weights, dprobs, top, total, delta


def fetch_kernel(heads, tiles, lists_hbm, counts_hbm, q_hbm, k_hbm, v_hbm, g_hbm,
                 stats_ref, table_out, far_tops_ref, far_weights_ref, far_dprobs_ref, q_ref, k_ref, v_ref, g_ref,
                 lists_ref, counts_ref, table, sem, table_sem):
    me = lax.axis_index("ctx")
    blocks_here = k_ref.shape[0]
    pieces = [
        (lists_hbm, lists_ref), (counts_hbm, counts_ref),
        (k_hbm, k_ref), (v_hbm, v_ref), (q_hbm, q_ref), (g_hbm, g_ref),
    ]
    fetches = [pltpu.make_async_copy(source, target, sem.at[i]) for i, (source, target) in enumerate(pieces)]
    for fetch in fetches:
        fetch.start()
    stats_ref[:, 0] = jnp.full_like(stats_ref[:, 0], MASKED)
    stats_ref[:, 1] = jnp.zeros_like(stats_ref[:, 1])
    stats_ref[:, 2] = jnp.zeros_like(stats_ref[:, 2])
    fetches[0].wait()
    fetches[1].wait()
    table_out[...] = slot_table(lists_ref[...], counts_ref[...], me, blocks_here)
    copy = pltpu.make_async_copy(table_out, table, table_sem)
    copy.start()
    copy.wait()
    for fetch in fetches[2:]:
        fetch.wait()

    def far(item, carry):
        row = table[item, QUEUE]
        head = row // tiles
        tile = lax.rem(row, tiles)
        group, place = seat(head, tile)
        weights, dprobs, top, total, delta = slot_stats(
            heads, tiles, table, q_ref, k_ref, v_ref, g_ref, head, tile, NEAR, MOST - NEAR
        )
        far_weights_ref[item] = weights
        far_dprobs_ref[item] = dprobs
        far_tops_ref[item] = top
        stats_ref[group, 0, place, :] = top
        stats_ref[group, 1, place, :] = total
        stats_ref[group, 2, place, :] = delta
        return carry

    lax.fori_loop(0, table[0, LENGTH], far, 0)


def join_kernel(n_ctx, heads, tiles, segments, table, far_ref, q_ref, k_ref, v_ref, g_ref,
                out_ref, acc_ref, tops_ref, weights_ref, dprobs_ref, stats_ref, zbuf, ybuf, part, merged, send1, recv1, send2, recv2, send3, recv3):
    me = lax.axis_index("ctx")
    head = lax.axis_index("head")
    n_z = n_ctx // Y
    z = me // Y
    y = lax.rem(me, Y)
    far_first = sorted(range(1, n_z), key=lambda i: -min(i, n_z - i))
    barrier = pltpu.get_barrier_semaphore()
    for i in far_first:
        pl.semaphore_signal(barrier, inc=1, device_id=(lax.rem(z + i, n_z) * Y + y, head), device_id_type=MESH)
    for i in range(1, Y):
        pl.semaphore_signal(barrier, inc=1, device_id=(z * Y + lax.rem(y + i, Y), head), device_id_type=MESH)

    def near(step):
        group = lax.rem(z + step, n_z)
        for inner in range(PAIR):
            for part_head in range(heads):
                tile = group * PAIR + inner
                row = part_head * tiles + tile
                place = pl.ds(part_head * PAIR + inner, 1)
                weights, dprobs, top, total, delta = slot_stats(
                    heads, tiles, table, q_ref, k_ref, v_ref, g_ref, part_head, tile, 0, NEAR
                )
                weights_ref[row] = weights
                dprobs_ref[row] = dprobs
                tops_ref[group, place, :] = top
                stats_ref[group, 1, place, :] = total
                stats_ref[group, 2, place, :] = delta

    def merge(step):
        group = lax.rem(z + step, n_z)
        tops = tops_ref[group]
        others = far_ref[group, 0]
        joint = jnp.maximum(tops, others)
        here = jnp.exp2(tops - joint)
        there = jnp.exp2(others - joint)
        stats_ref[group, 0] = joint
        for kind in (1, 2):
            stats_ref[group, kind] = here * stats_ref[group, kind] + there * far_ref[group, kind]


    def first(i, source):
        peer = lax.rem(z + i, n_z)
        return pltpu.make_async_remote_copy(
            src_ref=stats_ref.at[peer], dst_ref=zbuf.at[source], send_sem=send1.at[i], recv_sem=recv1.at[source],
            device_id=(peer * Y + y, head), device_id_type=MESH,
        )

    def second(i, source):
        peer = lax.rem(y + i, Y)
        return pltpu.make_async_remote_copy(
            src_ref=part, dst_ref=ybuf.at[source], send_sem=send2.at[i], recv_sem=recv2.at[source],
            device_id=(z * Y + peer, head), device_id_type=MESH,
        )

    def third(i, source):
        peer = lax.rem(z + i, n_z)
        return pltpu.make_async_remote_copy(
            src_ref=merged.at[source], dst_ref=merged.at[source], send_sem=send3.at[i], recv_sem=recv3.at[source],
            device_id=(peer * Y + y, head), device_id_type=MESH,
        )

    def combine(pieces):
        tops = pieces[:, 0]
        top = jnp.max(tops, axis=0)
        share = jnp.exp2(tops - top[None])
        return top, jnp.sum(share * pieces[:, 1], axis=0), jnp.sum(share * pieces[:, 2], axis=0)

    order = far_first + [0]
    for begin in range(0, n_z, n_z // segments):
        steps = order[begin : begin + n_z // segments]
        for i in steps:
            near(i)
        for i in steps:
            merge(i)
        if begin == 0:
            pl.semaphore_wait(barrier, n_z + Y - 2)
        for i in steps:
            if i > 0:
                first(i, z).start()
    zbuf[z] = stats_ref[z]
    acc_ref[...] = jnp.zeros_like(acc_ref)
    for i in range(1, n_z):
        first(i, lax.rem(z + i, n_z)).wait_recv()
    for kind, value in enumerate(combine(zbuf[...])):
        part[kind] = value
    for i in (2, 1, 3):
        second(i, y).start()
    ybuf[y] = part[...]
    for i in range(1, Y):
        second(i, lax.rem(y + i, Y)).wait_recv()
    top, total, delta = combine(ybuf[...])
    merged[z, 0] = top + jnp.log2(total)
    merged[z, 1] = delta / total
    for i in far_first:
        third(i, z).start()
    for i in range(1, n_z):
        first(i, z).wait_send()
    for i in range(1, Y):
        second(i, y).wait_send()
    for i in range(1, n_z):
        third(i, lax.rem(z + i, n_z)).wait_recv()
    out_ref[...] = merged[...]
    for i in range(1, n_z):
        third(i, z).wait_send()


def grads_kernel(heads, tiles, unroll, table, totals_ref, tops_ref, weights_ref, dprobs_ref,
                 far_tops_ref, far_weights_ref, far_dprobs_ref, q_ref, k_ref, g_ref, zeros_ref, dq_ref, acc):

    def spread(head, tile, group, place, first, probs, dprobs, keys):
        row = head * tiles + tile
        rows = span(tile, TILE)
        cols = span(head, HD)
        dscores = (probs * (dprobs - totals_ref[group, 1, place, :])).astype(BF16)
        both = jnp.concatenate([dscores, probs.astype(BF16)], axis=1)
        moved = dot_nn(both, diagonal(q_ref[rows, cols], g_ref[rows, cols]))
        for slot in range(keys.shape[0] // BLOCK):
            start = pl.multiple_of(table[row, first + slot] * BLOCK, BLOCK)
            acc[head, pl.ds(start, BLOCK), :] += moved[slot * BLOCK : (slot + 1) * BLOCK]
        return dscores

    for step in range(tiles // unroll):
        for inner in range(unroll):
            tile = step * unroll + inner
            rows = span(tile, TILE)
            pieces = []
            for head in range(heads):
                row = head * tiles + tile
                group, place = seat(head, tile)
                share = jnp.exp2(tops_ref[group, place, :] - totals_ref[group, 0, place, :])
                keys = picked(k_ref, table, row, head, 0, NEAR)
                dscores = spread(head, tile, group, place, 0, weights_ref[row] * share, dprobs_ref[row], keys)
                pieces.append((dscores, keys))
            moved = dot_tn(
                jnp.concatenate([pieces[0][0], pieces[1][0]], axis=0), diagonal(pieces[0][1], pieces[1][1])
            )
            dq_ref[rows, :] = (moved * SCALE).astype(BF16)

    def far(item, carry):
        row = table[item, QUEUE]
        head = row // tiles
        tile = lax.rem(row, tiles)
        group, place = seat(head, tile)
        rows = span(tile, TILE)
        cols = span(head, HD)
        share = jnp.exp2(far_tops_ref[item] - totals_ref[group, 0, place, :])
        keys = picked(k_ref, table, row, head, NEAR, MOST - NEAR)
        dscores = spread(head, tile, group, place, NEAR, far_weights_ref[item] * share, far_dprobs_ref[item], keys)
        extra = dot_tn(dscores, keys) * SCALE
        dq_ref[rows, cols] = (dq_ref[rows, cols].astype(F32) + extra).astype(BF16)
        return carry

    lax.fori_loop(0, table[0, LENGTH], far, 0)


def leave_kernel(count, *refs):
    sem = refs[2 * count]
    copies = [pltpu.make_async_copy(refs[i], refs[count + i], sem.at[i]) for i in range(count)]
    for copy in copies:
        copy.start()
    for copy in copies:
        copy.wait()


def swap_kernel(n_ctx, n_head, dq_ref, acc_ref, oq_ref, ok_ref, ov_ref, dk_ref, dv_ref,
                ybuf, zsend, zbuf, late_zbuf, late_send, late_ybuf,
                ssend, srecv, ysend, yrecv, zsend_sem, zrecv, late_zsend, late_zrecv, late_ysend, late_yrecv, own):
    me = lax.axis_index("ctx")
    head = lax.axis_index("head")
    n_z = n_ctx // Y
    z = me // Y
    y = lax.rem(me, Y)
    tokens = ok_ref.shape[0]
    width = dk_ref.shape[1]
    late = late_send.shape[1]
    early = oq_ref.shape[0] - late
    first_rows = pl.ds(0, early)
    last_rows = pl.ds(early, late)
    far_first = sorted(range(1, n_z), key=lambda i: -min(i, n_z - i))
    far_heads = sorted(range(1, n_head), key=lambda i: -min(i, n_head - i))
    order = far_first + [0]
    barrier = pltpu.get_barrier_semaphore()

    def at_head(i):
        return (me, lax.rem(head + i, n_head))

    def at_y(i):
        return (z * Y + lax.rem(y + i, Y), head)

    def at_z(i):
        return (lax.rem(z + i, n_z) * Y + y, head)

    for count, where in ((n_z, at_z), (n_head, at_head), (Y, at_y)):
        for i in range(1, count):
            pl.semaphore_signal(barrier, inc=1, device_id=where(i), device_id_type=MESH)
    for part in range(acc_ref.shape[0]):
        cols = pl.ds(part * HD, HD)
        dk_ref[:, cols] = (acc_ref[part, :, pl.ds(0, HD)] * SCALE).astype(BF16)
        dv_ref[:, cols] = acc_ref[part, :, pl.ds(HD, HD)].astype(BF16)
    pl.semaphore_wait(barrier, n_head + Y + n_z - 3)

    def token_copy(which, i, source):
        src, dst = ((dk_ref, ok_ref), (dv_ref, ov_ref))[which]
        peer = lax.rem(head + i, n_head)
        return pltpu.make_async_remote_copy(
            src_ref=src.at[pl.ds(pl.multiple_of(peer * tokens, tokens), tokens), :],
            dst_ref=dst.at[:, pl.ds(pl.multiple_of(source * width, width), width)],
            send_sem=ssend.at[which, i], recv_sem=srecv.at[which, source],
            device_id=(me, peer), device_id_type=MESH,
        )

    def y_copy(zz, i, source):
        peer = lax.rem(y + i, Y)
        return pltpu.make_async_remote_copy(
            src_ref=dq_ref.at[zz, peer, first_rows], dst_ref=ybuf.at[zz, source],
            send_sem=ysend.at[zz, i], recv_sem=yrecv.at[zz, source],
            device_id=(z * Y + peer, head), device_id_type=MESH,
        )

    def z_copy(i, source):
        peer = lax.rem(z + i, n_z)
        return pltpu.make_async_remote_copy(
            src_ref=zsend.at[peer], dst_ref=zbuf.at[source],
            send_sem=zsend_sem.at[i], recv_sem=zrecv.at[source],
            device_id=(peer * Y + y, head), device_id_type=MESH,
        )

    def late_z_copy(i, source):
        peer = lax.rem(z + i, n_z)
        return pltpu.make_async_remote_copy(
            src_ref=dq_ref.at[peer, :, last_rows], dst_ref=late_zbuf.at[source],
            send_sem=late_zsend.at[i], recv_sem=late_zrecv.at[source],
            device_id=(peer * Y + y, head), device_id_type=MESH,
        )

    def late_y_copy(i, source):
        peer = lax.rem(y + i, Y)
        return pltpu.make_async_remote_copy(
            src_ref=late_send.at[peer], dst_ref=late_ybuf.at[source],
            send_sem=late_ysend.at[i], recv_sem=late_yrecv.at[source],
            device_id=(z * Y + peer, head), device_id_type=MESH,
        )

    for i in far_heads:
        for which in range(2):
            token_copy(which, i, head).start()
    for i in far_first:
        late_z_copy(i, z).start()
    for i in order:
        zz = lax.rem(z + i, n_z)
        for j in (2, 1, 3):
            y_copy(zz, j, y).start()
    mine = []
    for which in range(2):
        src, dst = ((dk_ref, ok_ref), (dv_ref, ov_ref))[which]
        copy = pltpu.make_async_copy(
            src.at[pl.ds(pl.multiple_of(head * tokens, tokens), tokens), :],
            dst.at[:, pl.ds(pl.multiple_of(head * width, width), width)],
            own.at[which],
        )
        copy.start()
        mine.append(copy)

    for count, i in enumerate(order):
        zz = lax.rem(z + i, n_z)
        total = dq_ref[zz, y, first_rows].astype(F32)
        for j in range(1, Y):
            source = lax.rem(y + j, Y)
            y_copy(zz, j, source).wait_recv()
            total = total + ybuf[zz, source].astype(F32)
        if i > 0:
            zsend[zz] = total.astype(BF16)
            z_copy(i, z).start()
        if count == LATE_AFTER:
            crossed = dq_ref[z, :, last_rows].astype(F32)
            for j in range(1, n_z):
                source = lax.rem(z + j, n_z)
                late_z_copy(j, source).wait_recv()
                crossed = crossed + late_zbuf[source].astype(F32)
            late_send[...] = crossed.astype(BF16)
            for j in (2, 1, 3):
                late_y_copy(j, y).start()
    for i in range(1, n_z):
        source = lax.rem(z + i, n_z)
        z_copy(i, source).wait_recv()
        total = total + zbuf[source].astype(F32)
    oq_ref[first_rows, :] = total.astype(BF16)
    total = late_send[y].astype(F32)
    for j in range(1, Y):
        source = lax.rem(y + j, Y)
        late_y_copy(j, source).wait_recv()
        total = total + late_ybuf[source].astype(F32)
    oq_ref[last_rows, :] = total.astype(BF16)
    for copy in mine:
        copy.wait()
    for i in range(1, n_head):
        for which in range(2):
            token_copy(which, i, lax.rem(head + i, n_head)).wait_recv()
    for i in order:
        zz = lax.rem(z + i, n_z)
        for j in range(1, Y):
            y_copy(zz, j, y).wait_send()
    for i in range(1, n_z):
        z_copy(i, z).wait_send()
        late_z_copy(i, z).wait_send()
    for i in range(1, Y):
        late_y_copy(i, y).wait_send()
    for i in range(1, n_head):
        for which in range(2):
            token_copy(which, i, head).wait_send()


def local(n_ctx, n_head, queries, prefix_keys, prefix_values, out_grad, block_lists, list_counts):
    latents, width = queries.shape
    tokens = prefix_keys.shape[0]
    heads = width // HD
    tiles = latents // TILE
    rows = heads * tiles
    n_z = n_ctx // Y
    own = latents // n_ctx
    vmem = pl.BlockSpec(memory_space=pltpu.VMEM)
    smem = pl.BlockSpec(memory_space=pltpu.SMEM)
    hbm = pl.BlockSpec(memory_space=pltpu.HBM)
    prefix_keys = prefix_keys.reshape(tokens // BLOCK, BLOCK, width)
    prefix_values = prefix_values.reshape(tokens // BLOCK, BLOCK, width)
    operands = (block_lists, list_counts, queries, prefix_keys, prefix_values, out_grad)
    far_shape = (rows, (MOST - NEAR) * BLOCK, TILE)
    near_shape = (rows, NEAR * BLOCK, TILE)
    far_stats, table, *far_kept, queries, prefix_keys, prefix_values, out_grad = pl.pallas_call(
        functools.partial(fetch_kernel, heads, tiles),
        name="fetch",
        out_shape=(
            jax.ShapeDtypeStruct((n_z, 3, GROUP, TILE), F32),
            jax.ShapeDtypeStruct((rows, 128), jnp.int32),
            jax.ShapeDtypeStruct((rows, 1, TILE), F32),
            jax.ShapeDtypeStruct(far_shape, F32),
            jax.ShapeDtypeStruct(far_shape, F32),
            jax.ShapeDtypeStruct(queries.shape, BF16),
            jax.ShapeDtypeStruct(prefix_keys.shape, BF16),
            jax.ShapeDtypeStruct(prefix_values.shape, BF16),
            jax.ShapeDtypeStruct(out_grad.shape, BF16),
        ),
        in_specs=[hbm] * 6,
        out_specs=(vmem,) * 9,
        scratch_shapes=[
            pltpu.VMEM(block_lists.shape, jnp.int32),
            pltpu.VMEM(list_counts.shape, jnp.int32),
            pltpu.SMEM((rows, 128), jnp.int32),
            pltpu.SemaphoreType.DMA((6,)),
            pltpu.SemaphoreType.DMA,
        ],
        compiler_params=pltpu.CompilerParams(vmem_limit_bytes=VMEM_LIMIT),
    )(*[pltpu.with_memory_space_constraint(x, pltpu.HBM) for x in operands])
    totals, zeros, *near_kept = pl.pallas_call(
        functools.partial(join_kernel, n_ctx, heads, tiles, 4),
        name="join_stats",
        out_shape=(
            jax.ShapeDtypeStruct((n_z, 2, GROUP, TILE), F32),
            jax.ShapeDtypeStruct((heads, tokens, 2 * HD), F32),
            jax.ShapeDtypeStruct((n_z, GROUP, TILE), F32),
            jax.ShapeDtypeStruct(near_shape, F32),
            jax.ShapeDtypeStruct(near_shape, F32),
        ),
        in_specs=[smem] + [vmem] * 5,
        out_specs=(vmem,) * 5,
        scratch_shapes=[
            pltpu.VMEM((n_z, 3, GROUP, TILE), F32),
            pltpu.VMEM((n_z, 3, GROUP, TILE), F32),
            pltpu.VMEM((Y, 3, GROUP, TILE), F32),
            pltpu.VMEM((3, GROUP, TILE), F32),
            pltpu.VMEM((n_z, 2, GROUP, TILE), F32),
            pltpu.SemaphoreType.DMA((n_z,)),
            pltpu.SemaphoreType.DMA((n_z,)),
            pltpu.SemaphoreType.DMA((Y,)),
            pltpu.SemaphoreType.DMA((Y,)),
            pltpu.SemaphoreType.DMA((n_z,)),
            pltpu.SemaphoreType.DMA((n_z,)),
        ],
        compiler_params=pltpu.CompilerParams(collective_id=0, has_side_effects=True, vmem_limit_bytes=VMEM_LIMIT // 2),
    )(table, far_stats, queries, prefix_keys, prefix_values, out_grad)
    dq, acc = pl.pallas_call(
        functools.partial(grads_kernel, heads, tiles, 4),
        name="local_grads",
        out_shape=(
            jax.ShapeDtypeStruct((latents, width), BF16),
            jax.ShapeDtypeStruct((heads, tokens, 2 * HD), F32),
        ),
        in_specs=[smem] + [vmem] * 11,
        out_specs=(vmem, vmem),
        input_output_aliases={11: 1},
        compiler_params=pltpu.CompilerParams(vmem_limit_bytes=VMEM_LIMIT),
    )(table, totals, *near_kept, *far_kept, queries, prefix_keys, out_grad, zeros)
    piece = tokens // n_head
    results = pl.pallas_call(
        functools.partial(swap_kernel, n_ctx, n_head),
        name="swap_grads",
        out_shape=(
            jax.ShapeDtypeStruct((own, width), BF16),
            jax.ShapeDtypeStruct((piece, n_head * width), BF16),
            jax.ShapeDtypeStruct((piece, n_head * width), BF16),
        ),
        in_specs=[vmem, vmem],
        out_specs=(vmem, vmem, vmem),
        scratch_shapes=[
            pltpu.VMEM((tokens, width), BF16),
            pltpu.VMEM((tokens, width), BF16),
            pltpu.VMEM((n_z, Y, own - LATE, width), BF16),
            pltpu.VMEM((n_z, own - LATE, width), BF16),
            pltpu.VMEM((n_z, own - LATE, width), BF16),
            pltpu.VMEM((n_z, Y, LATE, width), BF16),
            pltpu.VMEM((Y, LATE, width), BF16),
            pltpu.VMEM((Y, LATE, width), BF16),
            pltpu.SemaphoreType.DMA((2, n_head)),
            pltpu.SemaphoreType.DMA((2, n_head)),
            pltpu.SemaphoreType.DMA((n_z, Y)),
            pltpu.SemaphoreType.DMA((n_z, Y)),
            pltpu.SemaphoreType.DMA((n_z,)),
            pltpu.SemaphoreType.DMA((n_z,)),
            pltpu.SemaphoreType.DMA((n_z,)),
            pltpu.SemaphoreType.DMA((n_z,)),
            pltpu.SemaphoreType.DMA((Y,)),
            pltpu.SemaphoreType.DMA((Y,)),
            pltpu.SemaphoreType.DMA((2,)),
        ],
        compiler_params=pltpu.CompilerParams(collective_id=1, has_side_effects=True, vmem_limit_bytes=VMEM_LIMIT // 2),
    )(dq.reshape(n_z, Y, own, width), acc)
    return pl.pallas_call(
        functools.partial(leave_kernel, len(results)),
        name="leave",
        out_shape=tuple(jax.ShapeDtypeStruct(result.shape, result.dtype) for result in results),
        in_specs=[vmem] * len(results),
        out_specs=(hbm,) * len(results),
        scratch_shapes=[pltpu.SemaphoreType.DMA((len(results),))],
        compiler_params=pltpu.CompilerParams(vmem_limit_bytes=VMEM_LIMIT),
    )(*results)


def solution(mesh):
    return jax.shard_map(
        functools.partial(local, mesh.shape["ctx"], mesh.shape["head"]),
        mesh=mesh,
        in_specs=(
            P(None, "head"),
            P("ctx", "head"),
            P("ctx", "head"),
            P(None, "head"),
            P("head", None, None),
            P("head", None),
        ),
        out_specs=(P("ctx", "head"), P(("ctx", "head"), None), P(("ctx", "head"), None)),
        check_vma=False,
    )
```

```python
import functools

import jax
import jax.numpy as jnp
from jax import lax
from jax.experimental import pallas as pl
from jax.experimental.pallas import tpu as pltpu
from jax.sharding import PartitionSpec as P

HD = 128
TILE = 128
BLOCK = 64
MOST = 8
NEAR = 2
Y = 4
GROUP = 4
PAIR = 2
LATE = 16
UNROLL = 16
QUEUE = MOST + 1
LENGTH = MOST + 2
LATE_AFTER = 5
MASKED = -1e30
SCALE = HD ** -0.5
SCALE2 = SCALE * 1.4426950408889634
MESH = pl.DeviceIdType.MESH
F32 = jnp.float32
BF16 = jnp.bfloat16
VMEM_LIMIT = 32 * 1024 * 1024


def dot_nt(a, b):
    return lax.dot_general(a, b, (((1,), (1,)), ((), ())), preferred_element_type=F32)


def dot_nn(a, b):
    return lax.dot_general(a, b, (((1,), (0,)), ((), ())), preferred_element_type=F32)


def dot_tn(a, b):
    return lax.dot_general(a, b, (((0,), (0,)), ((), ())), preferred_element_type=F32)


def span(index, size):
    start = index * size
    return pl.ds(start if isinstance(start, int) else pl.multiple_of(start, size), size)


def picked(ref, table, row, head, first, slots):
    cols = span(head, HD)
    return jnp.concatenate([ref[table[row, slot], :, cols] for slot in range(first, first + slots)], axis=0)


def slot_table(lists, counts_rows, me, blocks_here):
    heads, tiles, sel = lists.shape
    rows = heads * tiles
    eye = lax.broadcasted_iota(jnp.int32, (tiles, tiles), 0) == lax.broadcasted_iota(jnp.int32, (tiles, tiles), 1)
    counts = jnp.concatenate(
        [jnp.sum(jnp.where(eye, counts_rows[head : head + 1], 0), axis=1, keepdims=True) for head in range(heads)], axis=0
    )
    local = lists.reshape(rows, sel) - me * blocks_here
    pos = lax.broadcasted_iota(jnp.int32, (rows, sel), 1)
    listed = (pos < counts) & (local >= 0) & (local < blocks_here)
    flags = jnp.where(listed, 1.0, 0.0)
    before = lax.broadcasted_iota(jnp.int32, (sel, sel), 0) < lax.broadcasted_iota(jnp.int32, (sel, sel), 1)
    rank = dot_nn(flags.astype(BF16), jnp.where(before, 1.0, 0.0).astype(BF16))
    ids = local.astype(F32)
    lane = lax.broadcasted_iota(jnp.int32, (rows, 128), 1)
    total = jnp.sum(flags, axis=1, keepdims=True)
    more = jnp.where(total > float(NEAR), 1.0, 0.0)
    row = lax.broadcasted_iota(jnp.int32, (rows, 128), 0)
    above = lax.broadcasted_iota(jnp.int32, (rows, rows), 1) < lax.broadcasted_iota(jnp.int32, (rows, rows), 0)
    wide = jnp.broadcast_to(more, (rows, 128))
    order = dot_nn(jnp.where(above, 1.0, 0.0).astype(BF16), wide.astype(BF16))
    chosen = jnp.where((order == lane.astype(F32)) & (wide > 0.0), 1.0, 0.0)
    queue = dot_tn(chosen.astype(BF16), row.astype(F32).astype(BF16))[:rows]
    table = jnp.where(lane == MOST, total, 0.0)
    for slot in range(MOST):
        value = jnp.sum(jnp.where(listed & (rank == float(slot)), ids, 0.0), axis=1, keepdims=True)
        table = jnp.where(lane == slot, value, table)
    table = jnp.where(lane == QUEUE, queue, table)
    table = jnp.where(lane == LENGTH, jnp.sum(wide, axis=0, keepdims=True), table)
    return table.astype(jnp.int32)


def diagonal(a, b):
    zero = jnp.zeros_like(a)
    return jnp.concatenate([jnp.concatenate([a, zero], axis=1), jnp.concatenate([zero, b], axis=1)], axis=0)


def seat(head, tile):
    inner = tile % PAIR if isinstance(tile, int) else lax.rem(tile, PAIR)
    return tile // PAIR, pl.ds(head * PAIR + inner, 1)


def slot_stats(heads, tiles, table, q_ref, k_ref, v_ref, g_ref, head, tile, first, slots):
    row = head * tiles + tile
    live = (table[row, MOST] - first) * BLOCK
    rows = span(tile, TILE)
    cols = span(head, HD)
    keys = picked(k_ref, table, row, head, first, slots)
    vals = picked(v_ref, table, row, head, first, slots)
    scores = dot_nt(keys, q_ref[rows, cols]) * SCALE2
    dprobs = dot_nt(vals, g_ref[rows, cols])
    mask = lax.broadcasted_iota(jnp.int32, scores.shape, 0) < live
    scores = jnp.where(mask, scores, MASKED)
    top = jnp.max(scores, axis=0, keepdims=True)
    weights = jnp.where(mask, jnp.exp2(scores - top), 0.0)
    total = jnp.sum(weights, axis=0, keepdims=True)
    delta = jnp.sum(weights * dprobs, axis=0, keepdims=True)
    return weights, dprobs, top, total, delta


def fetch_kernel(heads, tiles, lists_hbm, counts_hbm, q_hbm, k_hbm, v_hbm, g_hbm,
                 stats_ref, table_out, far_tops_ref, far_weights_ref, far_dprobs_ref, q_ref, k_ref, v_ref, g_ref,
                 lists_ref, counts_ref, table, sem, table_sem):
    me = lax.axis_index("ctx")
    blocks_here = k_ref.shape[0]
    pieces = [
        (lists_hbm, lists_ref), (counts_hbm, counts_ref),
        (k_hbm, k_ref), (v_hbm, v_ref), (q_hbm, q_ref), (g_hbm, g_ref),
    ]
    fetches = [pltpu.make_async_copy(source, target, sem.at[i]) for i, (source, target) in enumerate(pieces)]
    for fetch in fetches:
        fetch.start()
    stats_ref[:, 0] = jnp.full_like(stats_ref[:, 0], MASKED)
    stats_ref[:, 1] = jnp.zeros_like(stats_ref[:, 1])
    stats_ref[:, 2] = jnp.zeros_like(stats_ref[:, 2])
    fetches[0].wait()
    fetches[1].wait()
    table_out[...] = slot_table(lists_ref[...], counts_ref[...], me, blocks_here)
    copy = pltpu.make_async_copy(table_out, table, table_sem)
    copy.start()
    copy.wait()
    for fetch in fetches[2:]:
        fetch.wait()

    def far(item, carry):
        row = table[item, QUEUE]
        head = row // tiles
        tile = lax.rem(row, tiles)
        group, place = seat(head, tile)
        weights, dprobs, top, total, delta = slot_stats(
            heads, tiles, table, q_ref, k_ref, v_ref, g_ref, head, tile, NEAR, MOST - NEAR
        )
        far_weights_ref[item] = weights
        far_dprobs_ref[item] = dprobs
        far_tops_ref[item] = top
        stats_ref[group, 0, place, :] = top
        stats_ref[group, 1, place, :] = total
        stats_ref[group, 2, place, :] = delta
        return carry

    def two(step, carry):
        far(2 * step, 0)
        far(2 * step + 1, 0)
        return carry

    lax.fori_loop(0, lax.div(table[0, LENGTH] + 1, 2), two, 0)


def join_kernel(n_ctx, heads, tiles, segments, table, far_ref, q_ref, k_ref, v_ref, g_ref,
                out_ref, acc_ref, tops_ref, weights_ref, dprobs_ref, stats_ref, zbuf, ybuf, part, merged, send1, recv1, send2, recv2, send3, recv3):
    me = lax.axis_index("ctx")
    head = lax.axis_index("head")
    n_z = n_ctx // Y
    z = me // Y
    y = lax.rem(me, Y)
    far_first = sorted(range(1, n_z), key=lambda i: -min(i, n_z - i))
    barrier = pltpu.get_barrier_semaphore()
    for i in far_first:
        pl.semaphore_signal(barrier, inc=1, device_id=(lax.rem(z + i, n_z) * Y + y, head), device_id_type=MESH)
    for i in range(1, Y):
        pl.semaphore_signal(barrier, inc=1, device_id=(z * Y + lax.rem(y + i, Y), head), device_id_type=MESH)

    def near(step):
        group = lax.rem(z + step, n_z)
        for inner in range(PAIR):
            for part_head in range(heads):
                tile = group * PAIR + inner
                row = part_head * tiles + tile
                place = pl.ds(part_head * PAIR + inner, 1)
                weights, dprobs, top, total, delta = slot_stats(
                    heads, tiles, table, q_ref, k_ref, v_ref, g_ref, part_head, tile, 0, NEAR
                )
                weights_ref[row] = weights
                dprobs_ref[row] = dprobs
                tops_ref[group, place, :] = top
                stats_ref[group, 1, place, :] = total
                stats_ref[group, 2, place, :] = delta

    def merge(step):
        group = lax.rem(z + step, n_z)
        tops = tops_ref[group]
        others = far_ref[group, 0]
        joint = jnp.maximum(tops, others)
        here = jnp.exp2(tops - joint)
        there = jnp.exp2(others - joint)
        stats_ref[group, 0] = joint
        for kind in (1, 2):
            stats_ref[group, kind] = here * stats_ref[group, kind] + there * far_ref[group, kind]


    def first(i, source):
        peer = lax.rem(z + i, n_z)
        return pltpu.make_async_remote_copy(
            src_ref=stats_ref.at[peer], dst_ref=zbuf.at[source], send_sem=send1.at[i], recv_sem=recv1.at[source],
            device_id=(peer * Y + y, head), device_id_type=MESH,
        )

    def second(i, source):
        peer = lax.rem(y + i, Y)
        return pltpu.make_async_remote_copy(
            src_ref=part, dst_ref=ybuf.at[source], send_sem=send2.at[i], recv_sem=recv2.at[source],
            device_id=(z * Y + peer, head), device_id_type=MESH,
        )

    def third(i, source):
        peer = lax.rem(z + i, n_z)
        return pltpu.make_async_remote_copy(
            src_ref=merged.at[source], dst_ref=merged.at[source], send_sem=send3.at[i], recv_sem=recv3.at[source],
            device_id=(peer * Y + y, head), device_id_type=MESH,
        )

    def combine(pieces):
        tops = pieces[:, 0]
        top = jnp.max(tops, axis=0)
        share = jnp.exp2(tops - top[None])
        return top, jnp.sum(share * pieces[:, 1], axis=0), jnp.sum(share * pieces[:, 2], axis=0)

    order = far_first + [0]
    for begin in range(0, n_z, n_z // segments):
        steps = order[begin : begin + n_z // segments]
        for i in steps:
            near(i)
        for i in steps:
            merge(i)
        if begin == 0:
            pl.semaphore_wait(barrier, n_z + Y - 2)
        for i in steps:
            if i > 0:
                first(i, z).start()
    zbuf[z] = stats_ref[z]
    acc_ref[...] = jnp.zeros_like(acc_ref)
    for i in range(1, n_z):
        first(i, lax.rem(z + i, n_z)).wait_recv()
    for kind, value in enumerate(combine(zbuf[...])):
        part[kind] = value
    for i in (2, 1, 3):
        second(i, y).start()
    ybuf[y] = part[...]
    for i in range(1, Y):
        second(i, lax.rem(y + i, Y)).wait_recv()
    top, total, delta = combine(ybuf[...])
    merged[z, 0] = top + jnp.log2(total)
    merged[z, 1] = delta / total
    for i in far_first:
        third(i, z).start()
    for i in range(1, n_z):
        first(i, z).wait_send()
    for i in range(1, Y):
        second(i, y).wait_send()
    for i in range(1, n_z):
        third(i, lax.rem(z + i, n_z)).wait_recv()
    out_ref[...] = merged[...]
    for i in range(1, n_z):
        third(i, z).wait_send()


def grads_kernel(heads, tiles, unroll, table, totals_ref, tops_ref, weights_ref, dprobs_ref,
                 far_tops_ref, far_weights_ref, far_dprobs_ref, q_ref, k_ref, g_ref, zeros_ref, dq_ref, acc):

    def spread(head, tile, group, place, first, probs, dprobs, keys):
        row = head * tiles + tile
        rows = span(tile, TILE)
        cols = span(head, HD)
        dscores = (probs * (dprobs - totals_ref[group, 1, place, :])).astype(BF16)
        both = jnp.concatenate([dscores, probs.astype(BF16)], axis=1)
        moved = dot_nn(both, diagonal(q_ref[rows, cols], g_ref[rows, cols]))
        for slot in range(keys.shape[0] // BLOCK):
            start = pl.multiple_of(table[row, first + slot] * BLOCK, BLOCK)
            acc[head, pl.ds(start, BLOCK), :] += moved[slot * BLOCK : (slot + 1) * BLOCK]
        return dscores

    for step in range(tiles // unroll):
        for inner in range(unroll):
            tile = step * unroll + inner
            rows = span(tile, TILE)
            pieces = []
            for head in range(heads):
                row = head * tiles + tile
                group, place = seat(head, tile)
                share = jnp.exp2(tops_ref[group, place, :] - totals_ref[group, 0, place, :])
                keys = picked(k_ref, table, row, head, 0, NEAR)
                dscores = spread(head, tile, group, place, 0, weights_ref[row] * share, dprobs_ref[row], keys)
                pieces.append((dscores, keys))
            moved = dot_tn(
                jnp.concatenate([pieces[0][0], pieces[1][0]], axis=0), diagonal(pieces[0][1], pieces[1][1])
            )
            dq_ref[rows, :] = (moved * SCALE).astype(BF16)

    def far(item, carry):
        row = table[item, QUEUE]
        head = row // tiles
        tile = lax.rem(row, tiles)
        group, place = seat(head, tile)
        rows = span(tile, TILE)
        cols = span(head, HD)
        share = jnp.exp2(far_tops_ref[item] - totals_ref[group, 0, place, :])
        share = jnp.where(item < table[0, LENGTH], share, 0.0)
        keys = picked(k_ref, table, row, head, NEAR, MOST - NEAR)
        dscores = spread(head, tile, group, place, NEAR, far_weights_ref[item] * share, far_dprobs_ref[item], keys)
        extra = dot_tn(dscores, keys) * SCALE
        dq_ref[rows, cols] = (dq_ref[rows, cols].astype(F32) + extra).astype(BF16)
        return carry

    def two(step, carry):
        far(2 * step, 0)
        far(2 * step + 1, 0)
        return carry

    lax.fori_loop(0, lax.div(table[0, LENGTH] + 1, 2), two, 0)


def leave_kernel(count, *refs):
    sem = refs[2 * count]
    copies = [pltpu.make_async_copy(refs[i], refs[count + i], sem.at[i]) for i in range(count)]
    for copy in copies:
        copy.start()
    for copy in copies:
        copy.wait()


def swap_kernel(n_ctx, n_head, dq_ref, acc_ref, oq_ref, ok_ref, ov_ref, dk_ref, dv_ref,
                ybuf, zsend, zbuf, late_zbuf, late_send, late_ybuf,
                ssend, srecv, ysend, yrecv, zsend_sem, zrecv, late_zsend, late_zrecv, late_ysend, late_yrecv, own):
    me = lax.axis_index("ctx")
    head = lax.axis_index("head")
    n_z = n_ctx // Y
    z = me // Y
    y = lax.rem(me, Y)
    tokens = ok_ref.shape[0]
    width = dk_ref.shape[1]
    late = late_send.shape[1]
    early = oq_ref.shape[0] - late
    first_rows = pl.ds(0, early)
    last_rows = pl.ds(early, late)
    far_first = sorted(range(1, n_z), key=lambda i: -min(i, n_z - i))
    far_heads = sorted(range(1, n_head), key=lambda i: -min(i, n_head - i))
    order = far_first + [0]
    barrier = pltpu.get_barrier_semaphore()

    def at_head(i):
        return (me, lax.rem(head + i, n_head))

    def at_y(i):
        return (z * Y + lax.rem(y + i, Y), head)

    def at_z(i):
        return (lax.rem(z + i, n_z) * Y + y, head)

    for count, where in ((n_z, at_z), (n_head, at_head), (Y, at_y)):
        for i in range(1, count):
            pl.semaphore_signal(barrier, inc=1, device_id=where(i), device_id_type=MESH)
    for part in range(acc_ref.shape[0]):
        cols = pl.ds(part * HD, HD)
        dk_ref[:, cols] = (acc_ref[part, :, pl.ds(0, HD)] * SCALE).astype(BF16)
        dv_ref[:, cols] = acc_ref[part, :, pl.ds(HD, HD)].astype(BF16)
    pl.semaphore_wait(barrier, n_head + Y + n_z - 3)

    def token_copy(which, i, source):
        src, dst = ((dk_ref, ok_ref), (dv_ref, ov_ref))[which]
        peer = lax.rem(head + i, n_head)
        return pltpu.make_async_remote_copy(
            src_ref=src.at[pl.ds(pl.multiple_of(peer * tokens, tokens), tokens), :],
            dst_ref=dst.at[:, pl.ds(pl.multiple_of(source * width, width), width)],
            send_sem=ssend.at[which, i], recv_sem=srecv.at[which, source],
            device_id=(me, peer), device_id_type=MESH,
        )

    def y_copy(zz, i, source):
        peer = lax.rem(y + i, Y)
        return pltpu.make_async_remote_copy(
            src_ref=dq_ref.at[zz, peer, first_rows], dst_ref=ybuf.at[zz, source],
            send_sem=ysend.at[zz, i], recv_sem=yrecv.at[zz, source],
            device_id=(z * Y + peer, head), device_id_type=MESH,
        )

    def z_copy(i, source):
        peer = lax.rem(z + i, n_z)
        return pltpu.make_async_remote_copy(
            src_ref=zsend.at[peer], dst_ref=zbuf.at[source],
            send_sem=zsend_sem.at[i], recv_sem=zrecv.at[source],
            device_id=(peer * Y + y, head), device_id_type=MESH,
        )

    def late_z_copy(i, source):
        peer = lax.rem(z + i, n_z)
        return pltpu.make_async_remote_copy(
            src_ref=dq_ref.at[peer, :, last_rows], dst_ref=late_zbuf.at[source],
            send_sem=late_zsend.at[i], recv_sem=late_zrecv.at[source],
            device_id=(peer * Y + y, head), device_id_type=MESH,
        )

    def late_y_copy(i, source):
        peer = lax.rem(y + i, Y)
        return pltpu.make_async_remote_copy(
            src_ref=late_send.at[peer], dst_ref=late_ybuf.at[source],
            send_sem=late_ysend.at[i], recv_sem=late_yrecv.at[source],
            device_id=(z * Y + peer, head), device_id_type=MESH,
        )

    for i in far_heads:
        for which in range(2):
            token_copy(which, i, head).start()
    for i in far_first:
        late_z_copy(i, z).start()
    for i in order:
        zz = lax.rem(z + i, n_z)
        for j in (2, 1, 3):
            y_copy(zz, j, y).start()
    mine = []
    for which in range(2):
        src, dst = ((dk_ref, ok_ref), (dv_ref, ov_ref))[which]
        copy = pltpu.make_async_copy(
            src.at[pl.ds(pl.multiple_of(head * tokens, tokens), tokens), :],
            dst.at[:, pl.ds(pl.multiple_of(head * width, width), width)],
            own.at[which],
        )
        copy.start()
        mine.append(copy)

    for count, i in enumerate(order):
        zz = lax.rem(z + i, n_z)
        total = dq_ref[zz, y, first_rows].astype(F32)
        for j in range(1, Y):
            source = lax.rem(y + j, Y)
            y_copy(zz, j, source).wait_recv()
            total = total + ybuf[zz, source].astype(F32)
        if i > 0:
            zsend[zz] = total.astype(BF16)
            z_copy(i, z).start()
        if count == LATE_AFTER:
            crossed = dq_ref[z, :, last_rows].astype(F32)
            for j in range(1, n_z):
                source = lax.rem(z + j, n_z)
                late_z_copy(j, source).wait_recv()
                crossed = crossed + late_zbuf[source].astype(F32)
            late_send[...] = crossed.astype(BF16)
            for j in (2, 1, 3):
                late_y_copy(j, y).start()
    for i in range(1, n_z):
        source = lax.rem(z + i, n_z)
        z_copy(i, source).wait_recv()
        total = total + zbuf[source].astype(F32)
    oq_ref[first_rows, :] = total.astype(BF16)
    total = late_send[y].astype(F32)
    for j in range(1, Y):
        source = lax.rem(y + j, Y)
        late_y_copy(j, source).wait_recv()
        total = total + late_ybuf[source].astype(F32)
    oq_ref[last_rows, :] = total.astype(BF16)
    for copy in mine:
        copy.wait()
    for i in range(1, n_head):
        for which in range(2):
            token_copy(which, i, lax.rem(head + i, n_head)).wait_recv()
    for i in order:
        zz = lax.rem(z + i, n_z)
        for j in range(1, Y):
            y_copy(zz, j, y).wait_send()
    for i in range(1, n_z):
        z_copy(i, z).wait_send()
        late_z_copy(i, z).wait_send()
    for i in range(1, Y):
        late_y_copy(i, y).wait_send()
    for i in range(1, n_head):
        for which in range(2):
            token_copy(which, i, head).wait_send()


def local(n_ctx, n_head, queries, prefix_keys, prefix_values, out_grad, block_lists, list_counts):
    latents, width = queries.shape
    tokens = prefix_keys.shape[0]
    heads = width // HD
    tiles = latents // TILE
    rows = heads * tiles
    n_z = n_ctx // Y
    own = latents // n_ctx
    vmem = pl.BlockSpec(memory_space=pltpu.VMEM)
    smem = pl.BlockSpec(memory_space=pltpu.SMEM)
    hbm = pl.BlockSpec(memory_space=pltpu.HBM)
    prefix_keys = prefix_keys.reshape(tokens // BLOCK, BLOCK, width)
    prefix_values = prefix_values.reshape(tokens // BLOCK, BLOCK, width)
    operands = (block_lists, list_counts, queries, prefix_keys, prefix_values, out_grad)
    far_shape = (rows, (MOST - NEAR) * BLOCK, TILE)
    near_shape = (rows, NEAR * BLOCK, TILE)
    far_stats, table, *far_kept, queries, prefix_keys, prefix_values, out_grad = pl.pallas_call(
        functools.partial(fetch_kernel, heads, tiles),
        name="fetch",
        out_shape=(
            jax.ShapeDtypeStruct((n_z, 3, GROUP, TILE), F32),
            jax.ShapeDtypeStruct((rows, 128), jnp.int32),
            jax.ShapeDtypeStruct((rows, 1, TILE), F32),
            jax.ShapeDtypeStruct(far_shape, F32),
            jax.ShapeDtypeStruct(far_shape, F32),
            jax.ShapeDtypeStruct(queries.shape, BF16),
            jax.ShapeDtypeStruct(prefix_keys.shape, BF16),
            jax.ShapeDtypeStruct(prefix_values.shape, BF16),
            jax.ShapeDtypeStruct(out_grad.shape, BF16),
        ),
        in_specs=[hbm] * 6,
        out_specs=(vmem,) * 9,
        scratch_shapes=[
            pltpu.VMEM(block_lists.shape, jnp.int32),
            pltpu.VMEM(list_counts.shape, jnp.int32),
            pltpu.SMEM((rows, 128), jnp.int32),
            pltpu.SemaphoreType.DMA((6,)),
            pltpu.SemaphoreType.DMA,
        ],
        compiler_params=pltpu.CompilerParams(vmem_limit_bytes=VMEM_LIMIT),
    )(*[pltpu.with_memory_space_constraint(x, pltpu.HBM) for x in operands])
    totals, zeros, *near_kept = pl.pallas_call(
        functools.partial(join_kernel, n_ctx, heads, tiles, 4),
        name="join_stats",
        out_shape=(
            jax.ShapeDtypeStruct((n_z, 2, GROUP, TILE), F32),
            jax.ShapeDtypeStruct((heads, tokens, 2 * HD), F32),
            jax.ShapeDtypeStruct((n_z, GROUP, TILE), F32),
            jax.ShapeDtypeStruct(near_shape, F32),
            jax.ShapeDtypeStruct(near_shape, F32),
        ),
        in_specs=[smem] + [vmem] * 5,
        out_specs=(vmem,) * 5,
        scratch_shapes=[
            pltpu.VMEM((n_z, 3, GROUP, TILE), F32),
            pltpu.VMEM((n_z, 3, GROUP, TILE), F32),
            pltpu.VMEM((Y, 3, GROUP, TILE), F32),
            pltpu.VMEM((3, GROUP, TILE), F32),
            pltpu.VMEM((n_z, 2, GROUP, TILE), F32),
            pltpu.SemaphoreType.DMA((n_z,)),
            pltpu.SemaphoreType.DMA((n_z,)),
            pltpu.SemaphoreType.DMA((Y,)),
            pltpu.SemaphoreType.DMA((Y,)),
            pltpu.SemaphoreType.DMA((n_z,)),
            pltpu.SemaphoreType.DMA((n_z,)),
        ],
        compiler_params=pltpu.CompilerParams(collective_id=0, has_side_effects=True, vmem_limit_bytes=VMEM_LIMIT // 2),
    )(table, far_stats, queries, prefix_keys, prefix_values, out_grad)
    dq, acc = pl.pallas_call(
        functools.partial(grads_kernel, heads, tiles, 4),
        name="local_grads",
        out_shape=(
            jax.ShapeDtypeStruct((latents, width), BF16),
            jax.ShapeDtypeStruct((heads, tokens, 2 * HD), F32),
        ),
        in_specs=[smem] + [vmem] * 11,
        out_specs=(vmem, vmem),
        input_output_aliases={11: 1},
        compiler_params=pltpu.CompilerParams(vmem_limit_bytes=VMEM_LIMIT),
    )(table, totals, *near_kept, *far_kept, queries, prefix_keys, out_grad, zeros)
    piece = tokens // n_head
    results = pl.pallas_call(
        functools.partial(swap_kernel, n_ctx, n_head),
        name="swap_grads",
        out_shape=(
            jax.ShapeDtypeStruct((own, width), BF16),
            jax.ShapeDtypeStruct((piece, n_head * width), BF16),
            jax.ShapeDtypeStruct((piece, n_head * width), BF16),
        ),
        in_specs=[vmem, vmem],
        out_specs=(vmem, vmem, vmem),
        scratch_shapes=[
            pltpu.VMEM((tokens, width), BF16),
            pltpu.VMEM((tokens, width), BF16),
            pltpu.VMEM((n_z, Y, own - LATE, width), BF16),
            pltpu.VMEM((n_z, own - LATE, width), BF16),
            pltpu.VMEM((n_z, own - LATE, width), BF16),
            pltpu.VMEM((n_z, Y, LATE, width), BF16),
            pltpu.VMEM((Y, LATE, width), BF16),
            pltpu.VMEM((Y, LATE, width), BF16),
            pltpu.SemaphoreType.DMA((2, n_head)),
            pltpu.SemaphoreType.DMA((2, n_head)),
            pltpu.SemaphoreType.DMA((n_z, Y)),
            pltpu.SemaphoreType.DMA((n_z, Y)),
            pltpu.SemaphoreType.DMA((n_z,)),
            pltpu.SemaphoreType.DMA((n_z,)),
            pltpu.SemaphoreType.DMA((n_z,)),
            pltpu.SemaphoreType.DMA((n_z,)),
            pltpu.SemaphoreType.DMA((Y,)),
            pltpu.SemaphoreType.DMA((Y,)),
            pltpu.SemaphoreType.DMA((2,)),
        ],
        compiler_params=pltpu.CompilerParams(collective_id=1, has_side_effects=True, vmem_limit_bytes=VMEM_LIMIT // 2),
    )(dq.reshape(n_z, Y, own, width), acc)
    return pl.pallas_call(
        functools.partial(leave_kernel, len(results)),
        name="leave",
        out_shape=tuple(jax.ShapeDtypeStruct(result.shape, result.dtype) for result in results),
        in_specs=[vmem] * len(results),
        out_specs=(hbm,) * len(results),
        scratch_shapes=[pltpu.SemaphoreType.DMA((len(results),))],
        compiler_params=pltpu.CompilerParams(vmem_limit_bytes=VMEM_LIMIT),
    )(*results)


def solution(mesh):
    return jax.shard_map(
        functools.partial(local, mesh.shape["ctx"], mesh.shape["head"]),
        mesh=mesh,
        in_specs=(
            P(None, "head"),
            P("ctx", "head"),
            P("ctx", "head"),
            P(None, "head"),
            P("head", None, None),
            P("head", None),
        ),
        out_specs=(P("ctx", "head"), P(("ctx", "head"), None), P(("ctx", "head"), None)),
        check_vma=False,
    )
```

```python
import functools

import jax
import jax.numpy as jnp
from jax import lax
from jax.experimental import pallas as pl
from jax.experimental.pallas import tpu as pltpu
from jax.sharding import PartitionSpec as P

HD = 128
TILE = 128
BLOCK = 64
MOST = 8
NEAR = 2
Y = 4
GROUP = 4
PAIR = 2
PARTS = 4
LATE = 16
UNROLL = 16
QUEUE = MOST + 1
LENGTH = MOST + 2
LATE_AFTER = 5
MASKED = -1e30
SCALE = HD ** -0.5
SCALE2 = SCALE * 1.4426950408889634
MESH = pl.DeviceIdType.MESH
F32 = jnp.float32
BF16 = jnp.bfloat16
VMEM_LIMIT = 32 * 1024 * 1024


def dot_nt(a, b):
    return lax.dot_general(a, b, (((1,), (1,)), ((), ())), preferred_element_type=F32)


def dot_nn(a, b):
    return lax.dot_general(a, b, (((1,), (0,)), ((), ())), preferred_element_type=F32)


def dot_tn(a, b):
    return lax.dot_general(a, b, (((0,), (0,)), ((), ())), preferred_element_type=F32)


def span(index, size):
    start = index * size
    return pl.ds(start if isinstance(start, int) else pl.multiple_of(start, size), size)


def picked(ref, table, row, head, first, slots):
    cols = span(head, HD)
    return jnp.concatenate([ref[table[row, slot], :, cols] for slot in range(first, first + slots)], axis=0)


def slot_table(lists, counts_rows, me, blocks_here):
    heads, tiles, sel = lists.shape
    rows = heads * tiles
    eye = lax.broadcasted_iota(jnp.int32, (tiles, tiles), 0) == lax.broadcasted_iota(jnp.int32, (tiles, tiles), 1)
    counts = jnp.concatenate(
        [jnp.sum(jnp.where(eye, counts_rows[head : head + 1], 0), axis=1, keepdims=True) for head in range(heads)], axis=0
    )
    local = lists.reshape(rows, sel) - me * blocks_here
    pos = lax.broadcasted_iota(jnp.int32, (rows, sel), 1)
    listed = (pos < counts) & (local >= 0) & (local < blocks_here)
    flags = jnp.where(listed, 1.0, 0.0)
    before = lax.broadcasted_iota(jnp.int32, (sel, sel), 0) < lax.broadcasted_iota(jnp.int32, (sel, sel), 1)
    rank = dot_nn(flags.astype(BF16), jnp.where(before, 1.0, 0.0).astype(BF16))
    ids = local.astype(F32)
    lane = lax.broadcasted_iota(jnp.int32, (rows, 128), 1)
    total = jnp.sum(flags, axis=1, keepdims=True)
    more = jnp.where(total > float(NEAR), 1.0, 0.0)
    row = lax.broadcasted_iota(jnp.int32, (rows, 128), 0)
    above = lax.broadcasted_iota(jnp.int32, (rows, rows), 1) < lax.broadcasted_iota(jnp.int32, (rows, rows), 0)
    wide = jnp.broadcast_to(more, (rows, 128))
    order = dot_nn(jnp.where(above, 1.0, 0.0).astype(BF16), wide.astype(BF16))
    chosen = jnp.where((order == lane.astype(F32)) & (wide > 0.0), 1.0, 0.0)
    queue = dot_tn(chosen.astype(BF16), row.astype(F32).astype(BF16))[:rows]
    table = jnp.where(lane == MOST, total, 0.0)
    for slot in range(MOST):
        value = jnp.sum(jnp.where(listed & (rank == float(slot)), ids, 0.0), axis=1, keepdims=True)
        table = jnp.where(lane == slot, value, table)
    table = jnp.where(lane == QUEUE, queue, table)
    table = jnp.where(lane == LENGTH, jnp.sum(wide, axis=0, keepdims=True), table)
    return table.astype(jnp.int32)


def diagonal(a, b):
    zero = jnp.zeros_like(a)
    return jnp.concatenate([jnp.concatenate([a, zero], axis=1), jnp.concatenate([zero, b], axis=1)], axis=0)


def seat(head, tile):
    inner = tile % PAIR if isinstance(tile, int) else lax.rem(tile, PAIR)
    return tile // PAIR, pl.ds(head * PAIR + inner, 1)


def slot_stats(heads, tiles, table, q_ref, k_ref, v_ref, g_ref, head, tile, first, slots):
    row = head * tiles + tile
    live = (table[row, MOST] - first) * BLOCK
    rows = span(tile, TILE)
    cols = span(head, HD)
    keys = picked(k_ref, table, row, head, first, slots)
    vals = picked(v_ref, table, row, head, first, slots)
    scores = dot_nt(keys, q_ref[rows, cols]) * SCALE2
    dprobs = dot_nt(vals, g_ref[rows, cols])
    mask = lax.broadcasted_iota(jnp.int32, scores.shape, 0) < live
    scores = jnp.where(mask, scores, MASKED)
    top = jnp.max(scores, axis=0, keepdims=True)
    weights = jnp.where(mask, jnp.exp2(scores - top), 0.0)
    total = jnp.sum(weights, axis=0, keepdims=True)
    delta = jnp.sum(weights * dprobs, axis=0, keepdims=True)
    return weights, dprobs, top, total, delta


def fetch_kernel(heads, tiles, lists_hbm, counts_hbm, q_hbm, k_hbm, v_hbm, g_hbm,
                 stats_ref, table_out, far_tops_ref, far_weights_ref, far_dprobs_ref, q_ref, k_ref, v_ref, g_ref,
                 lists_ref, counts_ref, table, sem, table_sem):
    me = lax.axis_index("ctx")
    blocks_here = k_ref.shape[0]
    pieces = [
        (lists_hbm, lists_ref), (counts_hbm, counts_ref),
        (k_hbm, k_ref), (v_hbm, v_ref), (q_hbm, q_ref), (g_hbm, g_ref),
    ]
    fetches = [pltpu.make_async_copy(source, target, sem.at[i]) for i, (source, target) in enumerate(pieces)]
    for fetch in fetches:
        fetch.start()
    stats_ref[:, 0] = jnp.full_like(stats_ref[:, 0], MASKED)
    stats_ref[:, 1] = jnp.zeros_like(stats_ref[:, 1])
    stats_ref[:, 2] = jnp.zeros_like(stats_ref[:, 2])
    fetches[0].wait()
    fetches[1].wait()
    table_out[...] = slot_table(lists_ref[...], counts_ref[...], me, blocks_here)
    copy = pltpu.make_async_copy(table_out, table, table_sem)
    copy.start()
    copy.wait()
    for fetch in fetches[2:]:
        fetch.wait()

    def far(item, carry):
        row = table[item, QUEUE]
        head = row // tiles
        tile = lax.rem(row, tiles)
        group, place = seat(head, tile)
        weights, dprobs, top, total, delta = slot_stats(
            heads, tiles, table, q_ref, k_ref, v_ref, g_ref, head, tile, NEAR, MOST - NEAR
        )
        far_weights_ref[item] = weights
        far_dprobs_ref[item] = dprobs
        far_tops_ref[item] = top
        stats_ref[group, 0, place, :] = top
        stats_ref[group, 1, place, :] = total
        stats_ref[group, 2, place, :] = delta
        return carry

    def two(step, carry):
        far(2 * step, 0)
        far(2 * step + 1, 0)
        return carry

    lax.fori_loop(0, lax.div(table[0, LENGTH] + 1, 2), two, 0)


def join_kernel(n_ctx, heads, tiles, segments, table, far_ref, q_ref, k_ref, v_ref, g_ref,
                out_ref, acc_ref, tops_ref, weights_ref, dprobs_ref, stats_ref, zbuf, ybuf, part, merged, send1, recv1, send2, recv2, send3, recv3):
    me = lax.axis_index("ctx")
    head = lax.axis_index("head")
    n_z = n_ctx // Y
    z = me // Y
    y = lax.rem(me, Y)
    far_first = sorted(range(1, n_z), key=lambda i: -min(i, n_z - i))
    barrier = pltpu.get_barrier_semaphore()
    for i in far_first:
        pl.semaphore_signal(barrier, inc=1, device_id=(lax.rem(z + i, n_z) * Y + y, head), device_id_type=MESH)
    for i in range(1, Y):
        pl.semaphore_signal(barrier, inc=1, device_id=(z * Y + lax.rem(y + i, Y), head), device_id_type=MESH)

    def near(step):
        group = lax.rem(z + step, n_z)
        for inner in range(PAIR):
            for part_head in range(heads):
                tile = group * PAIR + inner
                row = part_head * tiles + tile
                place = pl.ds(part_head * PAIR + inner, 1)
                weights, dprobs, top, total, delta = slot_stats(
                    heads, tiles, table, q_ref, k_ref, v_ref, g_ref, part_head, tile, 0, NEAR
                )
                weights_ref[row] = weights
                dprobs_ref[row] = dprobs
                tops_ref[group, place, :] = top
                stats_ref[group, 1, place, :] = total
                stats_ref[group, 2, place, :] = delta

    def merge(step):
        group = lax.rem(z + step, n_z)
        tops = tops_ref[group]
        others = far_ref[group, 0]
        joint = jnp.maximum(tops, others)
        here = jnp.exp2(tops - joint)
        there = jnp.exp2(others - joint)
        stats_ref[group, 0] = joint
        for kind in (1, 2):
            stats_ref[group, kind] = here * stats_ref[group, kind] + there * far_ref[group, kind]


    def first(i, source):
        peer = lax.rem(z + i, n_z)
        return pltpu.make_async_remote_copy(
            src_ref=stats_ref.at[peer], dst_ref=zbuf.at[source], send_sem=send1.at[i], recv_sem=recv1.at[source],
            device_id=(peer * Y + y, head), device_id_type=MESH,
        )

    def second(i, source):
        peer = lax.rem(y + i, Y)
        return pltpu.make_async_remote_copy(
            src_ref=part, dst_ref=ybuf.at[source], send_sem=send2.at[i], recv_sem=recv2.at[source],
            device_id=(z * Y + peer, head), device_id_type=MESH,
        )

    def third(i, source):
        peer = lax.rem(z + i, n_z)
        return pltpu.make_async_remote_copy(
            src_ref=merged.at[source], dst_ref=merged.at[source], send_sem=send3.at[i], recv_sem=recv3.at[source],
            device_id=(peer * Y + y, head), device_id_type=MESH,
        )

    def combine(pieces):
        tops = pieces[:, 0]
        top = jnp.max(tops, axis=0)
        share = jnp.exp2(tops - top[None])
        return top, jnp.sum(share * pieces[:, 1], axis=0), jnp.sum(share * pieces[:, 2], axis=0)

    order = far_first + [0]
    for begin in range(0, n_z, n_z // segments):
        steps = order[begin : begin + n_z // segments]
        for i in steps:
            near(i)
        for i in steps:
            merge(i)
        if begin == 0:
            pl.semaphore_wait(barrier, n_z + Y - 2)
        for i in steps:
            if i > 0:
                first(i, z).start()
    zbuf[z] = stats_ref[z]
    acc_ref[...] = jnp.zeros_like(acc_ref)
    for i in range(1, n_z):
        first(i, lax.rem(z + i, n_z)).wait_recv()
    for kind, value in enumerate(combine(zbuf[...])):
        part[kind] = value
    for i in (2, 1, 3):
        second(i, y).start()
    ybuf[y] = part[...]
    for i in range(1, Y):
        second(i, lax.rem(y + i, Y)).wait_recv()
    top, total, delta = combine(ybuf[...])
    merged[z, 0] = top + jnp.log2(total)
    merged[z, 1] = delta / total
    for i in far_first:
        third(i, z).start()
    for i in range(1, n_z):
        first(i, z).wait_send()
    for i in range(1, Y):
        second(i, y).wait_send()
    for i in range(1, n_z):
        third(i, lax.rem(z + i, n_z)).wait_recv()
    out_ref[...] = merged[...]
    for i in range(1, n_z):
        third(i, z).wait_send()


def grads_kernel(heads, tiles, unroll, table, totals_ref, tops_ref, weights_ref, dprobs_ref,
                 far_tops_ref, far_weights_ref, far_dprobs_ref, q_ref, k_ref, g_ref, zeros_ref, dq_ref, acc):

    def spread(head, tile, group, place, first, probs, dprobs, keys):
        row = head * tiles + tile
        rows = span(tile, TILE)
        cols = span(head, HD)
        dscores = (probs * (dprobs - totals_ref[group, 1, place, :])).astype(BF16)
        both = jnp.concatenate([dscores, probs.astype(BF16)], axis=1)
        moved = dot_nn(both, diagonal(q_ref[rows, cols], g_ref[rows, cols]))
        for slot in range(keys.shape[0] // BLOCK):
            start = pl.multiple_of(table[row, first + slot] * BLOCK, BLOCK)
            acc[head, pl.ds(start, BLOCK), :] += moved[slot * BLOCK : (slot + 1) * BLOCK]
        return dscores

    for step in range(tiles // unroll):
        for inner in range(unroll):
            tile = step * unroll + inner
            rows = span(tile, TILE)
            pieces = []
            for head in range(heads):
                row = head * tiles + tile
                group, place = seat(head, tile)
                share = jnp.exp2(tops_ref[group, place, :] - totals_ref[group, 0, place, :])
                keys = picked(k_ref, table, row, head, 0, NEAR)
                dscores = spread(head, tile, group, place, 0, weights_ref[row] * share, dprobs_ref[row], keys)
                pieces.append((dscores, keys))
            moved = dot_tn(
                jnp.concatenate([pieces[0][0], pieces[1][0]], axis=0), diagonal(pieces[0][1], pieces[1][1])
            )
            dq_ref[rows, :] = (moved * SCALE).astype(BF16)

    def far(item, carry):
        row = table[item, QUEUE]
        head = row // tiles
        tile = lax.rem(row, tiles)
        group, place = seat(head, tile)
        rows = span(tile, TILE)
        cols = span(head, HD)
        share = jnp.exp2(far_tops_ref[item] - totals_ref[group, 0, place, :])
        share = jnp.where(item < table[0, LENGTH], share, 0.0)
        keys = picked(k_ref, table, row, head, NEAR, MOST - NEAR)
        dscores = spread(head, tile, group, place, NEAR, far_weights_ref[item] * share, far_dprobs_ref[item], keys)
        extra = dot_tn(dscores, keys) * SCALE
        dq_ref[rows, cols] = (dq_ref[rows, cols].astype(F32) + extra).astype(BF16)
        return carry

    def two(step, carry):
        far(2 * step, 0)
        far(2 * step + 1, 0)
        return carry

    lax.fori_loop(0, lax.div(table[0, LENGTH] + 1, 2), two, 0)


def leave_kernel(count, *refs):
    sem = refs[2 * count]
    copies = []
    for i in range(count):
        part = refs[i].shape[0] // PARTS
        for j in range(PARTS):
            rows = pl.ds(j * part, part)
            copies.append(pltpu.make_async_copy(refs[i].at[rows], refs[count + i].at[rows], sem.at[i, j]))
    for copy in copies:
        copy.start()
    for copy in copies:
        copy.wait()


def swap_kernel(n_ctx, n_head, dq_ref, acc_ref, oq_ref, ok_ref, ov_ref, dk_ref, dv_ref,
                ybuf, zsend, zbuf, late_zbuf, late_send, late_ybuf,
                ssend, srecv, ysend, yrecv, zsend_sem, zrecv, late_zsend, late_zrecv, late_ysend, late_yrecv, own):
    me = lax.axis_index("ctx")
    head = lax.axis_index("head")
    n_z = n_ctx // Y
    z = me // Y
    y = lax.rem(me, Y)
    tokens = ok_ref.shape[0]
    width = dk_ref.shape[1]
    late = late_send.shape[1]
    early = oq_ref.shape[0] - late
    first_rows = pl.ds(0, early)
    last_rows = pl.ds(early, late)
    far_first = sorted(range(1, n_z), key=lambda i: -min(i, n_z - i))
    far_heads = sorted(range(1, n_head), key=lambda i: -min(i, n_head - i))
    order = far_first + [0]
    barrier = pltpu.get_barrier_semaphore()

    def at_head(i):
        return (me, lax.rem(head + i, n_head))

    def at_y(i):
        return (z * Y + lax.rem(y + i, Y), head)

    def at_z(i):
        return (lax.rem(z + i, n_z) * Y + y, head)

    for count, where in ((n_z, at_z), (n_head, at_head), (Y, at_y)):
        for i in range(1, count):
            pl.semaphore_signal(barrier, inc=1, device_id=where(i), device_id_type=MESH)
    for part in range(acc_ref.shape[0]):
        cols = pl.ds(part * HD, HD)
        dk_ref[:, cols] = (acc_ref[part, :, pl.ds(0, HD)] * SCALE).astype(BF16)
        dv_ref[:, cols] = acc_ref[part, :, pl.ds(HD, HD)].astype(BF16)
    pl.semaphore_wait(barrier, n_head + Y + n_z - 3)

    def token_copy(which, i, source):
        src, dst = ((dk_ref, ok_ref), (dv_ref, ov_ref))[which]
        peer = lax.rem(head + i, n_head)
        return pltpu.make_async_remote_copy(
            src_ref=src.at[pl.ds(pl.multiple_of(peer * tokens, tokens), tokens), :],
            dst_ref=dst.at[:, pl.ds(pl.multiple_of(source * width, width), width)],
            send_sem=ssend.at[which, i], recv_sem=srecv.at[which, source],
            device_id=(me, peer), device_id_type=MESH,
        )

    def y_copy(zz, i, source):
        peer = lax.rem(y + i, Y)
        return pltpu.make_async_remote_copy(
            src_ref=dq_ref.at[zz, peer, first_rows], dst_ref=ybuf.at[zz, source],
            send_sem=ysend.at[zz, i], recv_sem=yrecv.at[zz, source],
            device_id=(z * Y + peer, head), device_id_type=MESH,
        )

    def z_copy(i, source):
        peer = lax.rem(z + i, n_z)
        return pltpu.make_async_remote_copy(
            src_ref=zsend.at[peer], dst_ref=zbuf.at[source],
            send_sem=zsend_sem.at[i], recv_sem=zrecv.at[source],
            device_id=(peer * Y + y, head), device_id_type=MESH,
        )

    def late_z_copy(i, source):
        peer = lax.rem(z + i, n_z)
        return pltpu.make_async_remote_copy(
            src_ref=dq_ref.at[peer, :, last_rows], dst_ref=late_zbuf.at[source],
            send_sem=late_zsend.at[i], recv_sem=late_zrecv.at[source],
            device_id=(peer * Y + y, head), device_id_type=MESH,
        )

    def late_y_copy(i, source):
        peer = lax.rem(y + i, Y)
        return pltpu.make_async_remote_copy(
            src_ref=late_send.at[peer], dst_ref=late_ybuf.at[source],
            send_sem=late_ysend.at[i], recv_sem=late_yrecv.at[source],
            device_id=(z * Y + peer, head), device_id_type=MESH,
        )

    for i in far_heads:
        for which in range(2):
            token_copy(which, i, head).start()
    for i in far_first:
        late_z_copy(i, z).start()
    for i in order:
        zz = lax.rem(z + i, n_z)
        for j in (2, 1, 3):
            y_copy(zz, j, y).start()
    mine = []
    for which in range(2):
        src, dst = ((dk_ref, ok_ref), (dv_ref, ov_ref))[which]
        copy = pltpu.make_async_copy(
            src.at[pl.ds(pl.multiple_of(head * tokens, tokens), tokens), :],
            dst.at[:, pl.ds(pl.multiple_of(head * width, width), width)],
            own.at[which],
        )
        copy.start()
        mine.append(copy)

    for count, i in enumerate(order):
        zz = lax.rem(z + i, n_z)
        total = dq_ref[zz, y, first_rows].astype(F32)
        for j in range(1, Y):
            source = lax.rem(y + j, Y)
            y_copy(zz, j, source).wait_recv()
            total = total + ybuf[zz, source].astype(F32)
        if i > 0:
            zsend[zz] = total.astype(BF16)
            z_copy(i, z).start()
        if count == LATE_AFTER:
            crossed = dq_ref[z, :, last_rows].astype(F32)
            for j in range(1, n_z):
                source = lax.rem(z + j, n_z)
                late_z_copy(j, source).wait_recv()
                crossed = crossed + late_zbuf[source].astype(F32)
            late_send[...] = crossed.astype(BF16)
            for j in (2, 1, 3):
                late_y_copy(j, y).start()
    for i in range(1, n_z):
        source = lax.rem(z + i, n_z)
        z_copy(i, source).wait_recv()
        total = total + zbuf[source].astype(F32)
    oq_ref[first_rows, :] = total.astype(BF16)
    total = late_send[y].astype(F32)
    for j in range(1, Y):
        source = lax.rem(y + j, Y)
        late_y_copy(j, source).wait_recv()
        total = total + late_ybuf[source].astype(F32)
    oq_ref[last_rows, :] = total.astype(BF16)
    for copy in mine:
        copy.wait()
    for i in range(1, n_head):
        for which in range(2):
            token_copy(which, i, lax.rem(head + i, n_head)).wait_recv()
    for i in order:
        zz = lax.rem(z + i, n_z)
        for j in range(1, Y):
            y_copy(zz, j, y).wait_send()
    for i in range(1, n_z):
        z_copy(i, z).wait_send()
        late_z_copy(i, z).wait_send()
    for i in range(1, Y):
        late_y_copy(i, y).wait_send()
    for i in range(1, n_head):
        for which in range(2):
            token_copy(which, i, head).wait_send()


def local(n_ctx, n_head, queries, prefix_keys, prefix_values, out_grad, block_lists, list_counts):
    latents, width = queries.shape
    tokens = prefix_keys.shape[0]
    heads = width // HD
    tiles = latents // TILE
    rows = heads * tiles
    n_z = n_ctx // Y
    own = latents // n_ctx
    vmem = pl.BlockSpec(memory_space=pltpu.VMEM)
    smem = pl.BlockSpec(memory_space=pltpu.SMEM)
    hbm = pl.BlockSpec(memory_space=pltpu.HBM)
    prefix_keys = prefix_keys.reshape(tokens // BLOCK, BLOCK, width)
    prefix_values = prefix_values.reshape(tokens // BLOCK, BLOCK, width)
    operands = (block_lists, list_counts, queries, prefix_keys, prefix_values, out_grad)
    far_shape = (rows, (MOST - NEAR) * BLOCK, TILE)
    near_shape = (rows, NEAR * BLOCK, TILE)
    far_stats, table, *far_kept, queries, prefix_keys, prefix_values, out_grad = pl.pallas_call(
        functools.partial(fetch_kernel, heads, tiles),
        name="fetch",
        out_shape=(
            jax.ShapeDtypeStruct((n_z, 3, GROUP, TILE), F32),
            jax.ShapeDtypeStruct((rows, 128), jnp.int32),
            jax.ShapeDtypeStruct((rows, 1, TILE), F32),
            jax.ShapeDtypeStruct(far_shape, F32),
            jax.ShapeDtypeStruct(far_shape, F32),
            jax.ShapeDtypeStruct(queries.shape, BF16),
            jax.ShapeDtypeStruct(prefix_keys.shape, BF16),
            jax.ShapeDtypeStruct(prefix_values.shape, BF16),
            jax.ShapeDtypeStruct(out_grad.shape, BF16),
        ),
        in_specs=[hbm] * 6,
        out_specs=(vmem,) * 9,
        scratch_shapes=[
            pltpu.VMEM(block_lists.shape, jnp.int32),
            pltpu.VMEM(list_counts.shape, jnp.int32),
            pltpu.SMEM((rows, 128), jnp.int32),
            pltpu.SemaphoreType.DMA((6,)),
            pltpu.SemaphoreType.DMA,
        ],
        compiler_params=pltpu.CompilerParams(vmem_limit_bytes=VMEM_LIMIT),
    )(*[pltpu.with_memory_space_constraint(x, pltpu.HBM) for x in operands])
    totals, zeros, *near_kept = pl.pallas_call(
        functools.partial(join_kernel, n_ctx, heads, tiles, 4),
        name="join_stats",
        out_shape=(
            jax.ShapeDtypeStruct((n_z, 2, GROUP, TILE), F32),
            jax.ShapeDtypeStruct((heads, tokens, 2 * HD), F32),
            jax.ShapeDtypeStruct((n_z, GROUP, TILE), F32),
            jax.ShapeDtypeStruct(near_shape, F32),
            jax.ShapeDtypeStruct(near_shape, F32),
        ),
        in_specs=[smem] + [vmem] * 5,
        out_specs=(vmem,) * 5,
        scratch_shapes=[
            pltpu.VMEM((n_z, 3, GROUP, TILE), F32),
            pltpu.VMEM((n_z, 3, GROUP, TILE), F32),
            pltpu.VMEM((Y, 3, GROUP, TILE), F32),
            pltpu.VMEM((3, GROUP, TILE), F32),
            pltpu.VMEM((n_z, 2, GROUP, TILE), F32),
            pltpu.SemaphoreType.DMA((n_z,)),
            pltpu.SemaphoreType.DMA((n_z,)),
            pltpu.SemaphoreType.DMA((Y,)),
            pltpu.SemaphoreType.DMA((Y,)),
            pltpu.SemaphoreType.DMA((n_z,)),
            pltpu.SemaphoreType.DMA((n_z,)),
        ],
        compiler_params=pltpu.CompilerParams(collective_id=0, has_side_effects=True, vmem_limit_bytes=VMEM_LIMIT // 2),
    )(table, far_stats, queries, prefix_keys, prefix_values, out_grad)
    dq, acc = pl.pallas_call(
        functools.partial(grads_kernel, heads, tiles, 4),
        name="local_grads",
        out_shape=(
            jax.ShapeDtypeStruct((latents, width), BF16),
            jax.ShapeDtypeStruct((heads, tokens, 2 * HD), F32),
        ),
        in_specs=[smem] + [vmem] * 11,
        out_specs=(vmem, vmem),
        input_output_aliases={11: 1},
        compiler_params=pltpu.CompilerParams(vmem_limit_bytes=VMEM_LIMIT),
    )(table, totals, *near_kept, *far_kept, queries, prefix_keys, out_grad, zeros)
    piece = tokens // n_head
    results = pl.pallas_call(
        functools.partial(swap_kernel, n_ctx, n_head),
        name="swap_grads",
        out_shape=(
            jax.ShapeDtypeStruct((own, width), BF16),
            jax.ShapeDtypeStruct((piece, n_head * width), BF16),
            jax.ShapeDtypeStruct((piece, n_head * width), BF16),
        ),
        in_specs=[vmem, vmem],
        out_specs=(vmem, vmem, vmem),
        scratch_shapes=[
            pltpu.VMEM((tokens, width), BF16),
            pltpu.VMEM((tokens, width), BF16),
            pltpu.VMEM((n_z, Y, own - LATE, width), BF16),
            pltpu.VMEM((n_z, own - LATE, width), BF16),
            pltpu.VMEM((n_z, own - LATE, width), BF16),
            pltpu.VMEM((n_z, Y, LATE, width), BF16),
            pltpu.VMEM((Y, LATE, width), BF16),
            pltpu.VMEM((Y, LATE, width), BF16),
            pltpu.SemaphoreType.DMA((2, n_head)),
            pltpu.SemaphoreType.DMA((2, n_head)),
            pltpu.SemaphoreType.DMA((n_z, Y)),
            pltpu.SemaphoreType.DMA((n_z, Y)),
            pltpu.SemaphoreType.DMA((n_z,)),
            pltpu.SemaphoreType.DMA((n_z,)),
            pltpu.SemaphoreType.DMA((n_z,)),
            pltpu.SemaphoreType.DMA((n_z,)),
            pltpu.SemaphoreType.DMA((Y,)),
            pltpu.SemaphoreType.DMA((Y,)),
            pltpu.SemaphoreType.DMA((2,)),
        ],
        compiler_params=pltpu.CompilerParams(collective_id=1, has_side_effects=True, vmem_limit_bytes=VMEM_LIMIT // 2),
    )(dq.reshape(n_z, Y, own, width), acc)
    return pl.pallas_call(
        functools.partial(leave_kernel, len(results)),
        name="leave",
        out_shape=tuple(jax.ShapeDtypeStruct(result.shape, result.dtype) for result in results),
        in_specs=[vmem] * len(results),
        out_specs=(hbm,) * len(results),
        scratch_shapes=[pltpu.SemaphoreType.DMA((len(results), PARTS))],
        compiler_params=pltpu.CompilerParams(vmem_limit_bytes=VMEM_LIMIT),
    )(*results)


def solution(mesh):
    return jax.shard_map(
        functools.partial(local, mesh.shape["ctx"], mesh.shape["head"]),
        mesh=mesh,
        in_specs=(
            P(None, "head"),
            P("ctx", "head"),
            P("ctx", "head"),
            P(None, "head"),
            P("head", None, None),
            P("head", None),
        ),
        out_specs=(P("ctx", "head"), P(("ctx", "head"), None), P(("ctx", "head"), None)),
        check_vma=False,
    )
```
